512 devices in a mesh: beam: 32 (over z, core), path: 4 (over x), gz: 4 (over y).
Axes of the slice: x: 4, y: 4, z: 16, core: 2. Of those that a mesh axis runs over, the one named last changes fastest.
Arguments:
- maps: float32 [8, 64, 256, 512], P(None, 'gz', 'beam', 'path'), may hold values from 0.02 to 1
- measured: float32 [8, 64, 256], P(None, 'gz', 'beam'), may hold values from 0 to 76.8
- beta_table: float32 [8, 8], replicated, may hold values from 0.3 to 2
- view: int32 [1], replicated, may hold values from 0 to 7
- kappa: float32 [16, 8], replicated, may hold values from 0.3 to 2
- line_of: int32 [8], replicated, may hold values from 0 to 15
- side: int32 [8], replicated, may hold values from 0 to 1, as said below
Outputs:
- emission: float32 [8, 64, 256], P(None, 'gz', 'beam')
- maps_out: float32 [8, 64, 256, 512], P(None, 'gz', 'beam', 'path')
- data_dual: float32 [8, 64, 256], P(None, 'gz', 'beam')
The draws below stay inside these ranges and needn't reach their ends.
Inputs may be any that keep to these rules, and one draw needn't show every extreme that they name: Exactly 4 elements have side 0.
All inputs are finite; a program needn't handle non-finite values.
Results may differ from the reference program's by a relative error of at most 0.0001.
Values sent between devices are 32-bit elements; how exact they have to be, the bound alone decides.
A program may use at most 64 MiB of HBM per device.

```python
import math
import jax
import jax.numpy as jnp
from jax import lax

E = 8
L = 16
V = 8
ITERS = 2
NX = 256
NY = 512
NZ = 64


def draw_side(key, part):
    order = jax.random.permutation(key, E)
    return (order < E // 2).astype(jnp.int32)


def sparse_rows(key):
    offset = jax.random.randint(jax.random.fold_in(key, 7), (), 0, 4)
    elem_ids = jnp.arange(E, dtype=jnp.int32)[:, None]
    run_ids = (jnp.arange(NZ, dtype=jnp.int32) // 4)[None, :]
    return (elem_ids + run_ids + offset) % 4 == 0


def draw_maps(key, part):
    sparse = sparse_rows(key)
    uniform_cells = jax.random.uniform(jax.random.fold_in(key, 1), (E, NZ, NX, NY), jnp.float32)
    regular = 0.02 * jnp.exp(jnp.log(50.0) * uniform_cells)
    low_level = 0.02
    high_level = 1.0
    patch_z = (NZ + 3) // 4
    patch_x = (NX + 3) // 4
    patch_y = (NY + 7) // 8
    patches = jax.random.uniform(jax.random.fold_in(key, 2), (E, patch_z, patch_x, patch_y), jnp.float32)
    spread = jnp.repeat(jnp.repeat(jnp.repeat(patches, 4, axis=1), 4, axis=2), 8, axis=3)
    spread = spread[:, :NZ, :NX, :NY]
    levels = jnp.where(spread < 0.4, high_level, low_level)
    return jnp.where(sparse[:, :, None, None], levels, regular).astype(jnp.float32)


def draw_measured(key, part):
    sparse = sparse_rows(key)
    uniform_rows = jax.random.uniform(jax.random.fold_in(key, 3), (E, NZ, NX), jnp.float32)
    low_rows = uniform_rows * (0.004 * NY)
    high_rows = uniform_rows * (0.15 * NY)
    return jnp.where(sparse[:, :, None], low_rows, high_rows).astype(jnp.float32)


def with_ends(result, own_key, low, high):
    place = [jax.random.randint(jax.random.fold_in(own_key, axis), (), 0, length) for axis, length in enumerate(result.shape)]
    main_axis = result.shape.index(max(result.shape))
    neighbour = place[:main_axis] + [(place[main_axis] + 1) % result.shape[main_axis]] + place[main_axis + 1:]
    return result.at[tuple(place)].set(low).at[tuple(neighbour)].set(high)


def setup_inputs(seed: int = 0) -> dict:
    splits = jax.random.split(jax.random.key(seed), 8)
    return {
        "maps": draw_maps(jax.random.fold_in(splits[7], 71), 0),
        "measured": draw_measured(jax.random.fold_in(splits[7], 71), 0),
        "beta_table": jnp.clip(jnp.exp(jax.random.uniform(splits[2], (V, E), jnp.float32, math.log(0.3), math.log(2.0))), 0.3, 2.0),
        "view": jax.random.randint(splits[3], (1,), 0, V).astype(jnp.int32),
        "kappa": jnp.clip(jnp.exp(jax.random.uniform(splits[4], (L, E), jnp.float32, math.log(0.3), math.log(2.0))), 0.3, 2.0),
        "line_of": with_ends(jax.random.randint(splits[5], (E,), 0, L), jax.random.fold_in(splits[5], 1), 0, L - 1).astype(jnp.int32),
        "side": draw_side(jax.random.fold_in(splits[7], 71), 0),
    }


LAM = 0.1
HIGHP = lax.Precision.HIGHEST


def exclusive(values, axis):
    running = jnp.cumsum(values, axis=axis)
    count = values.shape[axis]
    head = jnp.zeros_like(lax.slice_in_dim(values, 0, 1, axis=axis))
    return jnp.concatenate([head, lax.slice_in_dim(running, 0, count - 1, axis=axis)], axis=axis)


def reverse_exclusive(values, axis):
    return jnp.flip(exclusive(jnp.flip(values, axis), axis), axis)


def forward_diff(values, axis):
    count = values.shape[axis]
    ahead = lax.slice_in_dim(values, 1, count, axis=axis) - lax.slice_in_dim(values, 0, count - 1, axis=axis)
    tail = jnp.zeros_like(lax.slice_in_dim(values, 0, 1, axis=axis))
    return jnp.concatenate([ahead, tail], axis=axis)


def back_diff(duals, axis):
    count = duals.shape[axis]
    head = jnp.zeros_like(lax.slice_in_dim(duals, 0, 1, axis=axis))
    earlier = jnp.concatenate([head, lax.slice_in_dim(duals, 0, count - 1, axis=axis)], axis=axis)
    return earlier - duals


def reference(maps, measured, beta_table, view, kappa, line_of, side):
    pick = (jnp.arange(V, dtype=jnp.int32) == view[0]).astype(jnp.float32)
    beta = jnp.dot(pick, beta_table, precision=HIGHP)
    mu_in = jnp.einsum('e,ezxy->zxy', beta, maps, precision=HIGHP)
    att_in = jnp.exp(-exclusive(mu_in, 1) / NX)
    onehot = (line_of[:, None] == jnp.arange(L, dtype=jnp.int32)[None, :]).astype(jnp.float32)
    absorb = jnp.dot(onehot, kappa, precision=HIGHP)
    mu_out = jnp.einsum('ef,fzxy->ezxy', absorb, maps, precision=HIGHP)
    depth = jnp.where(side[:, None, None, None] == 0, exclusive(mu_out, 3), reverse_exclusive(mu_out, 3))
    weight = att_in[None] * jnp.exp(-depth / NY)
    proj = jnp.sum(weight * maps, axis=3)
    total = jnp.sum(weight, axis=3)
    sig_q = 1.0 / total
    tau = 1.0 / (weight + 6.0)
    current = maps
    extrap = maps
    data_dual = jnp.zeros_like(proj)
    dual_z = jnp.zeros_like(maps)
    dual_x = jnp.zeros_like(maps)
    dual_y = jnp.zeros_like(maps)
    for step in range(ITERS):
        image = proj if step == 0 else jnp.sum(weight * extrap, axis=3)
        data_dual = (data_dual + sig_q * (image - measured)) / (1.0 + sig_q)
        dual_z = jnp.clip(dual_z + 0.5 * forward_diff(extrap, 1), -LAM, LAM)
        dual_x = jnp.clip(dual_x + 0.5 * forward_diff(extrap, 2), -LAM, LAM)
        dual_y = jnp.clip(dual_y + 0.5 * forward_diff(extrap, 3), -LAM, LAM)
        adjoint = back_diff(dual_z, 1) + back_diff(dual_x, 2) + back_diff(dual_y, 3)
        updated = jnp.maximum(current - tau * (weight * data_dual[..., None] + adjoint), 0.0)
        extrap = 2.0 * updated - current
        current = updated
    return proj / NY, current, data_dual
```

```python
import functools

import jax
import jax.numpy as jnp
from jax import lax
from jax.experimental import pallas as pl
from jax.experimental.pallas import tpu as pltpu
from jax.sharding import PartitionSpec as P

LAM = 0.1
F32 = jnp.float32
E, Z, X, Y = 8, 16, 8, 128
K = E * Z
ROWS = K * X

M_S = 0
M_CORE = 4
M_V = 5
M_H0 = 13
M_H1 = 19
M_STRIP = 25
M_B = 28
M_C = 31
M_N = 34


def clip(v):
    return jnp.clip(v, -LAM, LAM)


def split3(v):
    hi = v.astype(jnp.bfloat16)
    rest = v - hi.astype(F32)
    mid = rest.astype(jnp.bfloat16)
    low = (rest - mid.astype(F32)).astype(jnp.bfloat16)
    return hi, mid, low


def kernel(
    nb, np_, nz,
    maps_h, meas_h, beta_s, view_s, kappa_s, line_s, side_s,
    emis_o, out_o, dd_o,
    maps_v, w_v, pre_v, px_v, py_v, pz_v, adj_v, tau_v, tw_v, base_v, u_v, ext_v, ins_v, meas_v,
    s_v, sr_v, m_v, mr_v, v_v, vr_v, att_v,
    xs_v, xr_v, zs_v, zr_v, ys_v, yr_v, qx_v,
    strip_g, b_g, c_g, tr_v,
    in_sem, send_sem, recv_sem, far_sem,
):
    b = lax.axis_index("beam")
    c = b // 2
    k = lax.rem(b, 2)
    me = lax.axis_index("path")
    g = lax.axis_index("gz")
    nc = nb // 2

    def chip(d, other=False):
        core = (1 - k) if other else k
        return {"beam": lax.rem(c + d + nc, nc) * 2 + core}

    partner = {"beam": c * 2 + (1 - k)}
    b_lo = {"beam": lax.rem(b + nb - 1, nb)}
    b_hi = {"beam": lax.rem(b + 1, nb)}
    g_lo = {"gz": lax.rem(g + nz - 1, nz)}
    g_hi = {"gz": lax.rem(g + 1, nz)}
    p_to = [{"path": lax.rem(me + r, np_)} for r in (1, 2, 3)]
    p_lo, p_hi = p_to[2], p_to[0]

    barrier = pltpu.get_barrier_semaphore()
    peers = [chip(d, o) for d in (3, -3, 2, -2, 1, -1) for o in (False, True)]
    peers += p_to + [g_lo, g_hi, partner]
    for p in peers:
        pl.semaphore_signal(barrier, 1, device_id=p)

    loads = []
    for e in range(E):
        cp = pltpu.make_async_copy(maps_h.at[pl.ds(e * 128, 128)], maps_v.at[pl.ds(e * 128, 128)], in_sem.at[e])
        cp.start()
        loads.append(cp)
    meas_cp = pltpu.make_async_copy(meas_h, meas_v, in_sem.at[E])
    meas_cp.start()

    copies = []

    def send(src, dst, n, to):
        cp = pltpu.make_async_remote_copy(src, dst, send_sem.at[n], recv_sem.at[n], device_id=to)
        cp.start()
        copies.append(cp)
        return cp

    lane = lax.broadcasted_iota(jnp.int32, (X, Y), 1)
    sub = lax.broadcasted_iota(jnp.int32, (X, Y), 0)
    lane3 = lax.broadcasted_iota(jnp.int32, (Z, X, Y), 2)
    sub3 = lax.broadcasted_iota(jnp.int32, (Z, X, Y), 1)

    def blk(ref, e):
        return ref[pl.ds(e * 128, 128), :].reshape(Z, X, Y)

    def put(ref, e, v3):
        ref[pl.ds(e * 128, 128), :] = v3.reshape(128, Y)

    def compact(e, r3):
        acc = jnp.zeros((X, Y), F32)
        for z in range(Z):
            acc = jnp.where(lane == e * Z + z, r3[z], acc)
        return acc

    def flag(cond):
        return cond.astype(F32)

    acc = None
    for e in range(E):
        loads[e].wait()
        t = blk(maps_v, e) * beta_s[view_s[0], e]
        acc = t if acc is None else acc + t
    slab = jnp.sum(acc, axis=1)
    s_v[...] = slab

    pl.semaphore_wait(barrier, len(peers))
    for d in (3, -3):
        for o in (False, True):
            pl.semaphore_signal(far_sem, 1, device_id=chip(d, o))
    s_cp = [send(s_v, sr_v.at[i], M_S + i, chip(d)) for i, d in ((1, 2), (3, -2), (0, 1), (2, -1))]

    inc = acc
    for sh in (1, 2, 4):
        inc = inc + jnp.where(sub3 >= sh, pltpu.roll(inc, sh, 1), 0.0)
    ins_v[...] = (inc - acc).reshape(128, Y) * (1.0 / (nb * X))

    def compact_faces(ref):
        lo = jnp.zeros((X, Y), F32)
        hi = jnp.zeros((X, Y), F32)
        for e in range(E):
            v = blk(ref, e)
            lo = lo + compact(e, v[:, :, 0:1])
            hi = hi + compact(e, v[:, :, Y - 1 : Y])
        return lo, hi

    def x_faces(ref, it):
        xs_v[it, 0] = ref[pl.ds(0, K, stride=X), :]
        xs_v[it, 1] = ref[pl.ds(X - 1, K, stride=X), :]
        return [
            send(xs_v.at[it, 0], xr_v.at[it, 1], M_H0 + 6 * it + 1, b_lo),
            send(xs_v.at[it, 1], xr_v.at[it, 0], M_H0 + 6 * it + 0, b_hi),
        ]

    def z_faces(ref, it):
        for e in range(E):
            zs_v[it, 0, pl.ds(e * X, X), :] = ref[pl.ds(e * 128, X), :]
            zs_v[it, 1, pl.ds(e * X, X), :] = ref[pl.ds(e * 128 + 120, X), :]
        return [
            send(zs_v.at[it, 0], zr_v.at[it, 1], M_H0 + 6 * it + 3, g_lo),
            send(zs_v.at[it, 1], zr_v.at[it, 0], M_H0 + 6 * it + 2, g_hi),
        ]

    def y_faces(lo, hi, it):
        ys_v[it, 0] = lo
        ys_v[it, 1] = hi
        return [
            send(ys_v.at[it, 0], yr_v.at[it, 1], M_H0 + 6 * it + 5, p_lo),
            send(ys_v.at[it, 1], yr_v.at[it, 0], M_H0 + 6 * it + 4, p_hi),
        ]

    upper = (
        lax.broadcasted_iota(jnp.int32, (Y, Y), 0) < lax.broadcasted_iota(jnp.int32, (Y, Y), 1)
    ).astype(jnp.bfloat16)

    def absorb(e, strip):
        mo = None
        for f in range(E):
            t = maps_v[pl.ds(f * 128, 128), :] * kappa_s[line_s[e], f]
            mo = t if mo is None else mo + t
        fwd = sum(jnp.dot(part, upper, preferred_element_type=F32) for part in split3(mo))
        far = side_s[e].astype(F32)
        pre_v[pl.ds(pl.multiple_of(e * 128, 128), 128), :] = (1.0 - 2.0 * far) * fwd - far * mo
        return strip + compact(e, jnp.sum(mo.reshape(Z, X, Y), axis=2, keepdims=True))

    strip = lax.fori_loop(0, E, absorb, jnp.zeros((X, Y), F32))
    strip_g[me] = strip
    strip_cp = [send(strip_g.at[me], strip_g.at[me], M_STRIP + i, p_to[i]) for i in range(3)]
    h0 = x_faces(maps_v, 0) + z_faces(maps_v, 0)
    my0, my1 = compact_faces(maps_v)
    h0 += y_faces(my0, my1, 0)

    for cp in s_cp:
        cp.wait_recv()
    slab = s_v[...]
    near = sr_v[0] * flag(c >= 1) + sr_v[1] * flag(c >= 2)
    wrap1 = sr_v[2] * flag(c == nc - 1)
    v_v[0] = slab + near
    v_v[1] = slab * flag(c <= nc - 3) + sr_v[2] * flag(c != nc - 2) + sr_v[3]
    pl.semaphore_wait(far_sem, 4)
    v_cp = []
    for i, (src, d) in enumerate(((0, 6), (1, -5), (0, 3), (1, -2))):
        for o in range(2):
            n = 2 * i + o
            v_cp.append(send(v_v.at[src], vr_v.at[n], M_V + n, chip(d, o == 1)))
    m_v[...] = near + wrap1 + slab * flag(k == 0)
    m_cp = send(m_v, mr_v, M_CORE, partner)
    own_line = near + wrap1

    def interior(v3, p0, e):
        def step(diff, p):
            return clip(0.5 * diff) if p is None else clip(blk(p, e) + 0.5 * diff)

        px = jnp.where(sub3 == X - 1, 0.0, step(pltpu.roll(v3, X - 1, 1) - v3, p0 and p0[0]))
        py = jnp.where(lane3 == Y - 1, 0.0, step(pltpu.roll(v3, Y - 1, 2) - v3, p0 and p0[1]))
        zero = jnp.zeros((1, X, Y), F32)
        diff = jnp.concatenate([v3[1:] - v3[:-1], zero], axis=0)
        pz = step(diff, p0 and p0[2])
        adj = (pltpu.roll(px, 1, 1) - px) + (pltpu.roll(py, 1, 2) - py)
        adj = adj + (jnp.concatenate([zero, pz[:-1]], axis=0) - jnp.concatenate([pz[:-1], zero], axis=0))
        return adj, px, py, pz

    def first_dual(e, _):
        e = pl.multiple_of(e * 128, 128) // 128
        adj, px, py, pz = interior(blk(maps_v, e), None, e)
        put(adj_v, e, adj)
        put(px_v, e, px)
        put(py_v, e, py)
        put(pz_v, e, pz)
        return 0

    lax.fori_loop(0, E, first_dual, 0)

    for cp in strip_cp:
        cp.wait_recv()
    side_row = jnp.zeros((X, Y), F32)
    for e in range(E):
        side_row = jnp.where(lane // Z == e, side_s[e].astype(F32), side_row)
    below = jnp.zeros((X, Y), F32)
    above = jnp.zeros((X, Y), F32)
    for r in range(4):
        below = below + strip_g[r] * flag(me > r)
        above = above + strip_g[r] * flag(me <= r)
    offset = jnp.where(side_row == 0.0, below, above)
    ny = np_ * Y
    for e in range(E):
        local = blk(pre_v, e)
        ins = ins_v[...].reshape(Z, X, Y)
        parts = []
        for z in range(Z):
            n = e * Z + z
            parts.append(jnp.exp(-(offset[:, n : n + 1] + local[z]) * (1.0 / ny) - ins[z]))
        put(pre_v, e, jnp.stack(parts))

    m_xlo, m_xhi = flag(b > 0), flag(b < nb - 1)
    m_zlo, m_zhi = flag(g > 0), flag(g < nz - 1)
    m_ylo, m_yhi = flag(me > 0), flag(me < np_ - 1)
    ymask = flag(lane == 0) - flag(lane == Y - 1)
    xmask = flag(sub == 0) - flag(sub == X - 1)

    def faces(it, hs, q):
        for cp in hs:
            cp.wait_recv()
        qx = (
            clip(q[0] + (0.5 * m_xlo) * (xs_v[it, 0] - xr_v[it, 0])),
            clip(q[1] + (0.5 * m_xhi) * (xr_v[it, 1] - xs_v[it, 1])),
        )
        qz = (
            clip(q[2] + (0.5 * m_zlo) * (zs_v[it, 0] - zr_v[it, 0])),
            clip(q[3] + (0.5 * m_zhi) * (zr_v[it, 1] - zs_v[it, 1])),
        )
        qy = (
            clip(q[4] + (0.5 * m_ylo) * (ys_v[it, 0] - yr_v[it, 0])),
            clip(q[5] + (0.5 * m_yhi) * (yr_v[it, 1] - ys_v[it, 1])),
        )
        return qx + qz + qy

    def boundary(e, q):
        shifted = pltpu.roll(q[5], Y - 1, 1)
        even = lax.rem(lane, 2) == 0
        pair = (jnp.where(even, q[4], shifted), jnp.where(even, shifted, q[4]))
        parts = []
        for z in range(Z):
            n = e * Z + z
            r = pair[n % 2]
            if n:
                r = pltpu.roll(r, Y - n, 1)
            lo = jnp.broadcast_to(qx_v[0, pl.ds(n, 1), :], (X, Y))
            hi = jnp.broadcast_to(qx_v[1, pl.ds(n, 1), :], (X, Y))
            t = r * ymask + jnp.where(sub == 0, lo, hi) * xmask
            if z == 0:
                t = t + q[2][e * X : (e + 1) * X]
            if z == Z - 1:
                t = t - q[3][e * X : (e + 1) * X]
            parts.append(t)
        return jnp.stack(parts)

    q0 = faces(0, h0, (0.0,) * 6)
    qx_v[0] = q0[0]
    qx_v[1] = q0[1]
    for e in range(E):
        put(adj_v, e, blk(adj_v, e) + boundary(e, q0))
    qz0 = (q0[2], q0[3])
    qy0 = (q0[4], q0[5])
    zs_v[2, 0] = qz0[0]
    zs_v[2, 1] = qz0[1]

    meas_cp.wait()
    ident = (
        lax.broadcasted_iota(jnp.int32, (X, X), 0) == lax.broadcasted_iota(jnp.int32, (X, X), 1)
    ).astype(F32)
    meas = lax.dot_general(
        ident, meas_v[...], (((1,), (1,)), ((), ())), precision=lax.Precision.HIGHEST, preferred_element_type=F32
    )

    m_cp.wait_recv()
    carry = own_line + mr_v[...]
    for i, need in ((2, 3), (3, 12), (1, 9), (0, 6)):
        for o in range(2):
            v_cp[2 * i + o].wait_recv()
        carry = carry + (vr_v[2 * i] + vr_v[2 * i + 1]) * flag(c >= need)
    att_v[...] = jnp.exp(carry * (-1.0 / (nb * X)))
    projs = jnp.zeros((X, Y), F32)
    totals = jnp.zeros((X, Y), F32)
    attb = jnp.stack([jnp.broadcast_to(att_v[pl.ds(z, 1), :], (X, Y)) for z in range(Z)])
    for e in range(E):
        w = blk(pre_v, e) * attb
        put(w_v, e, w)
        totals = totals + compact(e, jnp.sum(w, axis=2, keepdims=True))
        projs = projs + compact(e, jnp.sum(w * blk(maps_v, e), axis=2, keepdims=True))
    b_g[me, 0] = projs
    b_g[me, 1] = totals
    b_cp = [send(b_g.at[me], b_g.at[me], M_B + i, p_to[i]) for i in (1, 0, 2)]

    by0 = jnp.zeros((X, Y), F32)
    by1 = jnp.zeros((X, Y), F32)
    ty0 = jnp.zeros((X, Y), F32)
    ty1 = jnp.zeros((X, Y), F32)
    for e in range(E):
        w = blk(w_v, e)
        tau = 1.0 / (w + 6.0)
        tw = tau * w
        base = blk(maps_v, e) - tau * blk(adj_v, e)
        put(tau_v, e, tau)
        put(tw_v, e, tw)
        put(base_v, e, base)
        by0 = by0 + compact(e, base[:, :, 0:1])
        by1 = by1 + compact(e, base[:, :, Y - 1 : Y])
        ty0 = ty0 + compact(e, tw[:, :, 0:1])
        ty1 = ty1 + compact(e, tw[:, :, Y - 1 : Y])

    for cp in b_cp:
        cp.wait_recv()
    total = (b_g[0] + b_g[1]) + (b_g[2] + b_g[3])
    proj = total[0]
    sig = 1.0 / total[1]
    inv = 1.0 / (1.0 + sig)
    dd = sig * (proj - meas) * inv

    ey0 = 2.0 * jnp.maximum(by0 - ty0 * dd, 0.0) - ys_v[0, 0]
    ey1 = 2.0 * jnp.maximum(by1 - ty1 * dd, 0.0) - ys_v[0, 1]
    h1 = y_faces(ey0, ey1, 1)

    def spread(vec, e):
        return jnp.stack(
            [jnp.broadcast_to(vec[:, n : n + 1], (X, Y)) for n in range(e * Z, (e + 1) * Z)]
        )

    image = jnp.zeros((X, Y), F32)
    for e in range(E):
        u = jnp.maximum(blk(base_v, e) - blk(tw_v, e) * spread(dd, e), 0.0)
        ext = 2.0 * u - blk(maps_v, e)
        put(u_v, e, u)
        put(ext_v, e, ext)
        image = image + compact(e, jnp.sum(blk(w_v, e) * ext, axis=2, keepdims=True))
    c_g[me] = image
    c_cp = [send(c_g.at[me], c_g.at[me], M_C + i, p_to[i]) for i in (1, 0, 2)]
    h1 += x_faces(ext_v, 1) + z_faces(ext_v, 1)

    def to_rows(v):
        return lax.dot_general(
            v, ident, (((0,), (0,)), ((), ())), precision=lax.Precision.HIGHEST, preferred_element_type=F32
        )

    tr_v[0] = to_rows(proj * (1.0 / ny))
    emis_cp = pltpu.make_async_copy(tr_v.at[0], emis_o, in_sem.at[E])
    emis_cp.start()

    for e in range(E):
        adj, _, _, _ = interior(blk(ext_v, e), (px_v, py_v, pz_v), e)
        put(base_v, e, blk(u_v, e) - blk(tau_v, e) * adj)

    q1 = faces(1, h1, (qx_v[0], qx_v[1], zs_v[2, 0], zs_v[2, 1]) + qy0)
    qx_v[0] = q1[0]
    qx_v[1] = q1[1]
    for e in range(E):
        put(base_v, e, blk(base_v, e) - blk(tau_v, e) * boundary(e, q1))

    for cp in c_cp:
        cp.wait_recv()
    image = (c_g[0] + c_g[1]) + (c_g[2] + c_g[3])
    dd = (dd + sig * (image - meas)) * inv
    outs = []
    for e in range(E):
        put(u_v, e, jnp.maximum(blk(base_v, e) - blk(tw_v, e) * spread(dd, e), 0.0))
        cp = pltpu.make_async_copy(u_v.at[pl.ds(e * 128, 128)], out_o.at[pl.ds(e * 128, 128)], in_sem.at[e])
        cp.start()
        outs.append(cp)
    tr_v[1] = to_rows(dd)
    dd_cp = pltpu.make_async_copy(tr_v.at[1], dd_o, in_sem.at[E + 1])
    dd_cp.start()
    for cp in copies:
        cp.wait_send()
    emis_cp.wait()
    dd_cp.wait()
    for cp in outs:
        cp.wait()


def shards(maps, measured, beta_table, view, kappa, line_of, side):
    sizes = tuple(lax.axis_size(a) for a in ("beam", "path", "gz"))
    big = pltpu.VMEM((ROWS, Y), F32)
    scratch = [big] * 12 + [
        pltpu.VMEM((128, Y), F32),
        pltpu.VMEM((K, X), F32),
        pltpu.VMEM((Z, Y), F32),
        pltpu.VMEM((4, Z, Y), F32),
        pltpu.VMEM((Z, Y), F32),
        pltpu.VMEM((Z, Y), F32),
        pltpu.VMEM((2, Z, Y), F32),
        pltpu.VMEM((8, Z, Y), F32),
        pltpu.VMEM((Z, Y), F32),
        pltpu.VMEM((2, 2, K, Y), F32),
        pltpu.VMEM((2, 2, K, Y), F32),
        pltpu.VMEM((3, 2, E * X, Y), F32),
        pltpu.VMEM((2, 2, E * X, Y), F32),
        pltpu.VMEM((2, 2, X, Y), F32),
        pltpu.VMEM((2, 2, X, Y), F32),
        pltpu.VMEM((2, K, Y), F32),
        pltpu.VMEM((4, X, Y), F32),
        pltpu.VMEM((4, 2, X, Y), F32),
        pltpu.VMEM((4, X, Y), F32),
        pltpu.VMEM((2, K, X), F32),
        pltpu.SemaphoreType.DMA((E + 2,)),
        pltpu.SemaphoreType.DMA((M_N,)),
        pltpu.SemaphoreType.DMA((M_N,)),
        pltpu.SemaphoreType.REGULAR,
    ]
    anyspace = pl.BlockSpec(memory_space=pl.ANY)
    smem = pl.BlockSpec(memory_space=pltpu.SMEM)
    emission, out, dual = pl.pallas_call(
        functools.partial(kernel, *sizes),
        out_shape=(
            jax.ShapeDtypeStruct((K, X), F32),
            jax.ShapeDtypeStruct((ROWS, Y), F32),
            jax.ShapeDtypeStruct((K, X), F32),
        ),
        in_specs=[anyspace, anyspace] + [smem] * 5,
        out_specs=(anyspace,) * 3,
        scratch_shapes=scratch,
        compiler_params=pltpu.CompilerParams(collective_id=0, has_side_effects=True),
        name="xrf",
    )(maps.reshape(ROWS, Y), measured.reshape(K, X), beta_table, view, kappa, line_of, side)
    return (
        emission.reshape(E, Z, X),
        out.reshape(E, Z, X, Y),
        dual.reshape(E, Z, X),
    )


def solution(mesh):
    return jax.shard_map(
        shards,
        mesh=mesh,
        in_specs=(P(None, "gz", "beam", "path"), P(None, "gz", "beam"), P(), P(), P(), P(), P()),
        out_specs=(P(None, "gz", "beam"), P(None, "gz", "beam", "path"), P(None, "gz", "beam")),
        check_vma=False,
    )
```

```python
import functools

import jax
import jax.numpy as jnp
from jax import lax
from jax.experimental import pallas as pl
from jax.experimental.pallas import tpu as pltpu
from jax.sharding import PartitionSpec as P

LAM = 0.1
F32 = jnp.float32
E, Z, X, Y = 8, 16, 8, 128
K = E * Z
ROWS = K * X

M_S = 0
M_CORE = 2
M_V = 3
M_H0 = 7
M_H1 = 13
M_STRIP = 19
M_B = 22
M_C = 25
M_N = 28
EARLY = 8


def clip(v):
    return jnp.clip(v, -LAM, LAM)


def split3(v):
    hi = v.astype(jnp.bfloat16)
    rest = v - hi.astype(F32)
    mid = rest.astype(jnp.bfloat16)
    low = (rest - mid.astype(F32)).astype(jnp.bfloat16)
    return hi, mid, low


def kernel(
    nb, np_, nz,
    maps_h, meas_h, beta_h, view_h, kappa_h, line_h, side_h,
    emis_o, out_o, dd_o,
    maps_v, w_v, pre_v, px_v, py_v, pz_v, adj_v, tau_v, tw_v, base_v, u_v, ext_v, ins_v, meas_v,
    s_v, sr_v, m_v, mr_v, v_v, vr_v, att_v,
    xs_v, xr_v, zs_v, zr_v, ys_v, yr_v, qx_v,
    strip_g, b_g, c_g,
    beta_s, view_s, kappa_s, line_s, side_s,
    in_sem, send_sem, recv_sem, far_sem,
):
    b = lax.axis_index("beam")
    c = lax.div(b, 2)
    k = b - 2 * c
    me = lax.axis_index("path")
    g = lax.axis_index("gz")
    nc = nb // 2
    last = nc - 1

    def chip(d, other=False):
        core = (1 - k) if other else k
        return {"beam": (c + d) * 2 + core}

    def ring(axis, at, n):
        return {axis: jnp.where(at >= n, at - n, at)}

    partner = {"beam": c * 2 + (1 - k)}
    b_lo = {"beam": b - 1}
    b_hi = {"beam": b + 1}
    g_lo = ring("gz", g + nz - 1, nz)
    g_hi = ring("gz", g + 1, nz)
    p_to = [ring("path", me + r, np_) for r in (1, 2, 3)]
    p_lo, p_hi = p_to[2], p_to[0]

    barrier = pltpu.get_barrier_semaphore()

    def greet(p):
        pl.semaphore_signal(barrier, 1, device_id=p)

    def inside(d):
        return (c + d >= 0) & (c + d <= last)

    for p in p_to + [g_lo, g_hi, partner]:
        greet(p)
    for d in (-3, 3, -2, 2, -1, 1):
        @pl.when(inside(d))
        def _():
            greet(chip(d))
            greet(chip(d, True))
    met = 6 + 2 * (jnp.minimum(c, 3) + jnp.minimum(last - c, 3))

    loads = []
    for i, (src, dst) in enumerate(((beta_h, beta_s), (view_h, view_s))):
        cp = pltpu.make_async_copy(src, dst, in_sem.at[E + 1 + i])
        cp.start()
        loads.append(cp)
    tables = loads
    loads = []
    for e in range(E):
        cp = pltpu.make_async_copy(maps_h.at[pl.ds(e * 128, 128)], maps_v.at[pl.ds(e * 128, 128)], in_sem.at[e])
        cp.start()
        loads.append(cp)
    meas_cp = pltpu.make_async_copy(meas_h, meas_v, in_sem.at[E])
    meas_cp.start()
    lines = []
    for i, (src, dst) in enumerate(((kappa_h, kappa_s), (line_h, line_s), (side_h, side_s))):
        cp = pltpu.make_async_copy(src, dst, in_sem.at[E + 3 + i])
        cp.start()
        lines.append(cp)

    @pl.when(c < 1)
    def _():
        sr_v[0] = jnp.zeros((Z, Y), F32)

    @pl.when(c < 2)
    def _():
        sr_v[1] = jnp.zeros((Z, Y), F32)

    @pl.when(c < 3)
    def _():
        vr_v[0] = jnp.zeros((Z, Y), F32)
        vr_v[1] = jnp.zeros((Z, Y), F32)

    @pl.when(c < EARLY + 3)
    def _():
        vr_v[2] = jnp.zeros((Z, Y), F32)
        vr_v[3] = jnp.zeros((Z, Y), F32)

    @pl.when(b == 0)
    def _():
        for it in range(2):
            xr_v[it, 0] = jnp.zeros((K, Y), F32)

    @pl.when(b == nb - 1)
    def _():
        for it in range(2):
            xr_v[it, 1] = jnp.zeros((K, Y), F32)

    copies = []

    def send(src, dst, n, to, cond=None):
        cp = pltpu.make_async_remote_copy(src, dst, send_sem.at[n], recv_sem.at[n], device_id=to)
        if cond is None:
            cp.start()
        else:
            pl.when(cond)(cp.start)
        copies.append((cond, cp))
        return cp

    def arrive(cp, cond=None):
        if cond is None:
            cp.wait_recv()
        else:
            pl.when(cond)(cp.wait_recv)

    lane = lax.broadcasted_iota(jnp.int32, (X, Y), 1)
    sub = lax.broadcasted_iota(jnp.int32, (X, Y), 0)
    lane3 = lax.broadcasted_iota(jnp.int32, (Z, X, Y), 2)
    sub3 = lax.broadcasted_iota(jnp.int32, (Z, X, Y), 1)

    def blk(ref, e):
        return ref[pl.ds(e * 128, 128), :].reshape(Z, X, Y)

    def put(ref, e, v3):
        ref[pl.ds(e * 128, 128), :] = v3.reshape(128, Y)

    def compact(e, r3):
        acc = jnp.zeros((X, Y), F32)
        for z in range(Z):
            acc = jnp.where(lane == e * Z + z, r3[z], acc)
        return acc

    def flag(cond):
        return cond.astype(F32)

    for cp in tables:
        cp.wait()
    acc = None
    for e in range(E):
        loads[e].wait()
        t = blk(maps_v, e) * beta_s[view_s[0], e]
        acc = t if acc is None else acc + t
    slab = jnp.sum(acc, axis=1)
    s_v[...] = slab

    pl.semaphore_wait(barrier, met)

    @pl.when((c >= EARLY) & (c <= last - 3))
    def _():
        for o in (False, True):
            pl.semaphore_signal(far_sem, 1, device_id=chip(-3, o))

    s_cp = [send(s_v, sr_v.at[i], M_S + i, chip(i + 1), c + i + 1 <= last) for i in (1, 0)]
    s_cp.reverse()

    inc = acc
    for sh in (1, 2, 4):
        inc = inc + jnp.where(sub3 >= sh, pltpu.roll(inc, sh, 1), 0.0)
    ins_v[...] = (inc - acc).reshape(128, Y) * (1.0 / (nb * X))

    def compact_faces(ref):
        lo = jnp.zeros((X, Y), F32)
        hi = jnp.zeros((X, Y), F32)
        for e in range(E):
            v = blk(ref, e)
            lo = lo + compact(e, v[:, :, 0:1])
            hi = hi + compact(e, v[:, :, Y - 1 : Y])
        return lo, hi

    def x_faces(ref, it):
        xs_v[it, 0] = ref[pl.ds(0, K, stride=X), :]
        xs_v[it, 1] = ref[pl.ds(X - 1, K, stride=X), :]
        return [
            (send(xs_v.at[it, 0], xr_v.at[it, 1], M_H0 + 6 * it + 1, b_lo, b > 0), b < nb - 1),
            (send(xs_v.at[it, 1], xr_v.at[it, 0], M_H0 + 6 * it + 0, b_hi, b < nb - 1), b > 0),
        ]

    def z_faces(ref, it):
        for e in range(E):
            zs_v[it, 0, pl.ds(e * X, X), :] = ref[pl.ds(e * 128, X), :]
            zs_v[it, 1, pl.ds(e * X, X), :] = ref[pl.ds(e * 128 + 120, X), :]
        return [
            (send(zs_v.at[it, 0], zr_v.at[it, 1], M_H0 + 6 * it + 3, g_lo), None),
            (send(zs_v.at[it, 1], zr_v.at[it, 0], M_H0 + 6 * it + 2, g_hi), None),
        ]

    def y_faces(lo, hi, it):
        ys_v[it, 0] = lo
        ys_v[it, 1] = hi
        return [
            (send(ys_v.at[it, 0], yr_v.at[it, 1], M_H0 + 6 * it + 5, p_lo), None),
            (send(ys_v.at[it, 1], yr_v.at[it, 0], M_H0 + 6 * it + 4, p_hi), None),
        ]

    upper = (
        lax.broadcasted_iota(jnp.int32, (Y, Y), 0) < lax.broadcasted_iota(jnp.int32, (Y, Y), 1)
    ).astype(jnp.bfloat16)

    def absorb(e, strip):
        mo = None
        for f in range(E):
            t = maps_v[pl.ds(f * 128, 128), :] * kappa_s[f, line_s[e]]
            mo = t if mo is None else mo + t
        fwd = sum(jnp.dot(part, upper, preferred_element_type=F32) for part in split3(mo))
        far = side_s[e].astype(F32)
        pre_v[pl.ds(pl.multiple_of(e * 128, 128), 128), :] = (1.0 - 2.0 * far) * fwd - far * mo
        return strip + compact(e, jnp.sum(mo.reshape(Z, X, Y), axis=2, keepdims=True))

    for cp in lines:
        cp.wait()
    strip = lax.fori_loop(0, E, absorb, jnp.zeros((X, Y), F32))
    strip_g[me] = strip
    strip_cp = [send(strip_g.at[me], strip_g.at[me], M_STRIP + i, p_to[i]) for i in range(3)]
    h0 = x_faces(maps_v, 0) + z_faces(maps_v, 0)
    my0, my1 = compact_faces(maps_v)
    h0 += y_faces(my0, my1, 0)

    for i in range(2):
        arrive(s_cp[i], c >= i + 1)
    near = sr_v[0] + sr_v[1]
    v_v[0] = s_v[...] + near
    m_v[...] = near + s_v[...] * flag(k == 0)
    m_cp = send(m_v, mr_v, M_CORE, partner)

    def windows(src, at, d, cond):
        return [send(v_v.at[src], vr_v.at[at + o], M_V + at + o, chip(d, o == 1), cond) for o in range(2)]

    three = windows(0, 0, 3, (c < 3) | ((c >= EARLY) & (c <= last - 3)))
    mid = (c >= 3) & (c < EARLY)

    @pl.when(mid)
    def _():
        three[0].wait_recv()
        v_v[1] = v_v[0] + vr_v[0]

    three_mid = windows(1, 0, 3, mid)

    def interior(v3, p0, e):
        def step(diff, p):
            return clip(0.5 * diff) if p is None else clip(blk(p, e) + 0.5 * diff)

        px = jnp.where(sub3 == X - 1, 0.0, step(pltpu.roll(v3, X - 1, 1) - v3, p0 and p0[0]))
        py = jnp.where(lane3 == Y - 1, 0.0, step(pltpu.roll(v3, Y - 1, 2) - v3, p0 and p0[1]))
        zero = jnp.zeros((1, X, Y), F32)
        diff = jnp.concatenate([v3[1:] - v3[:-1], zero], axis=0)
        pz = step(diff, p0 and p0[2])
        adj = (pltpu.roll(px, 1, 1) - px) + (pltpu.roll(py, 1, 2) - py)
        adj = adj + (jnp.concatenate([zero, pz[:-1]], axis=0) - jnp.concatenate([pz[:-1], zero], axis=0))
        return adj, px, py, pz

    def first_dual(e, _):
        e = pl.multiple_of(e * 128, 128) // 128
        adj, px, py, pz = interior(blk(maps_v, e), None, e)
        put(adj_v, e, adj)
        put(px_v, e, px)
        put(py_v, e, py)
        put(pz_v, e, pz)
        return 0

    lax.fori_loop(0, E, first_dual, 0)

    for cp in strip_cp:
        cp.wait_recv()
    side_row = jnp.zeros((X, Y), F32)
    for e in range(E):
        side_row = jnp.where(lane // Z == e, side_s[e].astype(F32), side_row)
    below = jnp.zeros((X, Y), F32)
    above = jnp.zeros((X, Y), F32)
    for r in range(4):
        below = below + strip_g[r] * flag(me > r)
        above = above + strip_g[r] * flag(me <= r)
    offset = jnp.where(side_row == 0.0, below, above)
    ny = np_ * Y
    for e in range(E):
        local = blk(pre_v, e)
        ins = ins_v[...].reshape(Z, X, Y)
        parts = []
        for z in range(Z):
            n = e * Z + z
            parts.append(jnp.exp(-(offset[:, n : n + 1] + local[z]) * (1.0 / ny) - ins[z]))
        put(pre_v, e, jnp.stack(parts))

    m_xlo, m_xhi = flag(b > 0), flag(b < nb - 1)
    m_zlo, m_zhi = flag(g > 0), flag(g < nz - 1)
    m_ylo, m_yhi = flag(me > 0), flag(me < np_ - 1)
    ymask = flag(lane == 0) - flag(lane == Y - 1)
    xmask = flag(sub == 0) - flag(sub == X - 1)

    def faces(it, hs, q):
        for cp, cond in hs:
            arrive(cp, cond)
        qx = (
            clip(q[0] + (0.5 * m_xlo) * (xs_v[it, 0] - xr_v[it, 0])),
            clip(q[1] + (0.5 * m_xhi) * (xr_v[it, 1] - xs_v[it, 1])),
        )
        qz = (
            clip(q[2] + (0.5 * m_zlo) * (zs_v[it, 0] - zr_v[it, 0])),
            clip(q[3] + (0.5 * m_zhi) * (zr_v[it, 1] - zs_v[it, 1])),
        )
        qy = (
            clip(q[4] + (0.5 * m_ylo) * (ys_v[it, 0] - yr_v[it, 0])),
            clip(q[5] + (0.5 * m_yhi) * (yr_v[it, 1] - ys_v[it, 1])),
        )
        return qx + qz + qy

    def boundary(e, q):
        shifted = pltpu.roll(q[5], Y - 1, 1)
        even = lax.rem(lane, 2) == 0
        pair = (jnp.where(even, q[4], shifted), jnp.where(even, shifted, q[4]))
        parts = []
        for z in range(Z):
            n = e * Z + z
            r = pair[n % 2]
            if n:
                r = pltpu.roll(r, Y - n, 1)
            lo = jnp.broadcast_to(qx_v[0, pl.ds(n, 1), :], (X, Y))
            hi = jnp.broadcast_to(qx_v[1, pl.ds(n, 1), :], (X, Y))
            t = r * ymask + jnp.where(sub == 0, lo, hi) * xmask
            if z == 0:
                t = t + q[2][e * X : (e + 1) * X]
            if z == Z - 1:
                t = t - q[3][e * X : (e + 1) * X]
            parts.append(t)
        return jnp.stack(parts)

    q0 = faces(0, h0, (0.0,) * 6)
    qx_v[0] = q0[0]
    qx_v[1] = q0[1]
    for e in range(E):
        put(adj_v, e, blk(adj_v, e) + boundary(e, q0))
    qz0 = (q0[2], q0[3])
    qy0 = (q0[4], q0[5])
    zs_v[2, 0] = qz0[0]
    zs_v[2, 1] = qz0[1]

    meas_cp.wait()
    meas = jnp.zeros((X, Y), F32)
    for e in range(E):
        row = jnp.pad(meas_v[pl.ds(e * X, X), :], ((0, 0), (0, Y - Z)))
        meas = meas + (pltpu.roll(row, e * Z, 1) if e else row)

    late = (c >= EARLY) & (c <= last - 6)

    @pl.when(late)
    def _():
        three[0].wait_recv()
        v_v[1] = v_v[0] + vr_v[0]

    has_six = (c >= EARLY - 3) & (c <= last - 6)

    @pl.when(has_six)
    def _():
        pl.semaphore_wait(far_sem, 2)

    six = windows(1, 2, 6, has_six)
    arrive(m_cp)
    arrive(three[0], c > last - 6)
    arrive(three[1], c >= 3)
    for cp in six:
        arrive(cp, c >= EARLY + 3)
    carry = (sr_v[0] + sr_v[1] + mr_v[...]) + (vr_v[0] + vr_v[1]) + (vr_v[2] + vr_v[3])
    att_v[...] = jnp.exp(carry * (-1.0 / (nb * X)))
    projs = jnp.zeros((X, Y), F32)
    totals = jnp.zeros((X, Y), F32)
    attb = jnp.stack([jnp.broadcast_to(att_v[pl.ds(z, 1), :], (X, Y)) for z in range(Z)])
    for e in range(E):
        w = blk(pre_v, e) * attb
        put(w_v, e, w)
        totals = totals + compact(e, jnp.sum(w, axis=2, keepdims=True))
        projs = projs + compact(e, jnp.sum(w * blk(maps_v, e), axis=2, keepdims=True))
    b_g[me, 0] = projs
    b_g[me, 1] = totals
    b_cp = [send(b_g.at[me], b_g.at[me], M_B + i, p_to[i]) for i in (1, 0, 2)]

    by0 = jnp.zeros((X, Y), F32)
    by1 = jnp.zeros((X, Y), F32)
    ty0 = jnp.zeros((X, Y), F32)
    ty1 = jnp.zeros((X, Y), F32)
    for e in range(E):
        w = blk(w_v, e)
        tau = 1.0 / (w + 6.0)
        tw = tau * w
        base = blk(maps_v, e) - tau * blk(adj_v, e)
        put(tau_v, e, tau)
        put(tw_v, e, tw)
        put(base_v, e, base)
        by0 = by0 + compact(e, base[:, :, 0:1])
        by1 = by1 + compact(e, base[:, :, Y - 1 : Y])
        ty0 = ty0 + compact(e, tw[:, :, 0:1])
        ty1 = ty1 + compact(e, tw[:, :, Y - 1 : Y])

    for cp in b_cp:
        cp.wait_recv()
    total = (b_g[0] + b_g[1]) + (b_g[2] + b_g[3])
    proj = total[0]
    sig = 1.0 / total[1]
    inv = 1.0 / (1.0 + sig)
    dd = sig * (proj - meas) * inv

    ey0 = 2.0 * jnp.maximum(by0 - ty0 * dd, 0.0) - ys_v[0, 0]
    ey1 = 2.0 * jnp.maximum(by1 - ty1 * dd, 0.0) - ys_v[0, 1]
    h1 = y_faces(ey0, ey1, 1)

    def spread(vec, e):
        return jnp.stack(
            [jnp.broadcast_to(vec[:, n : n + 1], (X, Y)) for n in range(e * Z, (e + 1) * Z)]
        )

    image = jnp.zeros((X, Y), F32)
    for e in range(E):
        u = jnp.maximum(blk(base_v, e) - blk(tw_v, e) * spread(dd, e), 0.0)
        ext = 2.0 * u - blk(maps_v, e)
        put(u_v, e, u)
        put(ext_v, e, ext)
        image = image + compact(e, jnp.sum(blk(w_v, e) * ext, axis=2, keepdims=True))
    c_g[me] = image
    c_cp = [send(c_g.at[me], c_g.at[me], M_C + i, p_to[i]) for i in (1, 0, 2)]
    h1 += x_faces(ext_v, 1) + z_faces(ext_v, 1)

    def rows_out(ref, v):
        for e in range(E):
            turned = pltpu.roll(v, Y - e * Z, 1) if e else v
            ref[pl.ds(e * X, X), :] = turned[:, :Z]

    rows_out(emis_o, proj * (1.0 / ny))

    for e in range(E):
        adj, _, _, _ = interior(blk(ext_v, e), (px_v, py_v, pz_v), e)
        put(base_v, e, blk(u_v, e) - blk(tau_v, e) * adj)

    q1 = faces(1, h1, (qx_v[0], qx_v[1], zs_v[2, 0], zs_v[2, 1]) + qy0)
    qx_v[0] = q1[0]
    qx_v[1] = q1[1]
    for e in range(E):
        put(base_v, e, blk(base_v, e) - blk(tau_v, e) * boundary(e, q1))

    for cp in c_cp:
        cp.wait_recv()
    image = (c_g[0] + c_g[1]) + (c_g[2] + c_g[3])
    dd = (dd + sig * (image - meas)) * inv
    for e in range(E):
        put(out_o, e, jnp.maximum(blk(base_v, e) - blk(tw_v, e) * spread(dd, e), 0.0))
    rows_out(dd_o, dd)
    for cond, cp in copies:
        if cond is None:
            cp.wait_send()
        else:
            pl.when(cond)(cp.wait_send)


def shards(maps, measured, beta_table, view, kappa, line_of, side):
    sizes = tuple(lax.axis_size(a) for a in ("beam", "path", "gz"))
    big = pltpu.VMEM((ROWS, Y), F32)
    scratch = [big] * 12 + [
        pltpu.VMEM((128, Y), F32),
        pltpu.VMEM((E * X, Z), F32),
        pltpu.VMEM((Z, Y), F32),
        pltpu.VMEM((2, Z, Y), F32),
        pltpu.VMEM((Z, Y), F32),
        pltpu.VMEM((Z, Y), F32),
        pltpu.VMEM((2, Z, Y), F32),
        pltpu.VMEM((4, Z, Y), F32),
        pltpu.VMEM((Z, Y), F32),
        pltpu.VMEM((2, 2, K, Y), F32),
        pltpu.VMEM((2, 2, K, Y), F32),
        pltpu.VMEM((3, 2, E * X, Y), F32),
        pltpu.VMEM((2, 2, E * X, Y), F32),
        pltpu.VMEM((2, 2, X, Y), F32),
        pltpu.VMEM((2, 2, X, Y), F32),
        pltpu.VMEM((2, K, Y), F32),
        pltpu.VMEM((4, X, Y), F32),
        pltpu.VMEM((4, 2, X, Y), F32),
        pltpu.VMEM((4, X, Y), F32),
        pltpu.SMEM(beta_table.shape, F32),
        pltpu.SMEM(view.shape, jnp.int32),
        pltpu.SMEM(kappa.shape[::-1], F32),
        pltpu.SMEM(line_of.shape, jnp.int32),
        pltpu.SMEM(side.shape, jnp.int32),
        pltpu.SemaphoreType.DMA((E + 6,)),
        pltpu.SemaphoreType.DMA((M_N,)),
        pltpu.SemaphoreType.DMA((M_N,)),
        pltpu.SemaphoreType.REGULAR,
    ]
    emission, out, dual = pl.pallas_call(
        functools.partial(kernel, *sizes),
        out_shape=(
            pltpu.VMEM((E * X, Z), F32),
            pltpu.VMEM((ROWS, Y), F32),
            pltpu.VMEM((E * X, Z), F32),
        ),
        in_specs=[pl.BlockSpec(memory_space=pltpu.HBM)] * 7,
        scratch_shapes=scratch,
        compiler_params=pltpu.CompilerParams(collective_id=0, has_side_effects=True),
        name="xrf",
    )(
        maps.reshape(ROWS, Y),
        measured.transpose(0, 2, 1).reshape(E * X, Z),
        beta_table,
        view,
        kappa.T,
        line_of,
        side,
    )
    return (
        emission.reshape(E, X, Z).transpose(0, 2, 1),
        out.reshape(E, Z, X, Y),
        dual.reshape(E, X, Z).transpose(0, 2, 1),
    )


def solution(mesh):
    return jax.shard_map(
        shards,
        mesh=mesh,
        in_specs=(P(None, "gz", "beam", "path"), P(None, "gz", "beam"), P(), P(), P(), P(), P()),
        out_specs=(P(None, "gz", "beam"), P(None, "gz", "beam", "path"), P(None, "gz", "beam")),
        check_vma=False,
    )
```

```python
import functools

import jax
import jax.numpy as jnp
from jax import lax
from jax.experimental import pallas as pl
from jax.experimental.pallas import tpu as pltpu
from jax.sharding import PartitionSpec as P

LAM = 0.1
F32 = jnp.float32
E, Z, X, Y = 8, 16, 8, 128
K = E * Z
ROWS = K * X

M_S = 0
M_CORE = 2
M_V = 3
M_H0 = 11
M_H1 = 17
M_STRIP = 23
M_B = 26
M_C = 29
M_BACK = 32
M_N = 34
EARLY = 8


def clip(v):
    return jnp.clip(v, -LAM, LAM)


def split2(v):
    hi = v.astype(jnp.bfloat16)
    rest = v - hi.astype(F32)
    mid = rest.astype(jnp.bfloat16)
    return hi, mid


def kernel(
    nb, np_, nz,
    maps_h, meas_h, beta_h, view_h, kappa_h, line_h, side_h,
    emis_o, out_o, dd_o,
    maps_v, w_v, pre_v, px_v, py_v, pz_v, adj_v, tau_v, tw_v, base_v, u_v, ext_v, ins_v, meas_v,
    s_v, sr_v, m_v, mr_v, v_v, vr_v, bk_v, att_v,
    xs_v, xr_v, zs_v, zr_v, ys_v, yr_v, qx_v,
    strip_g, b_g, c_g,
    beta_s, view_s, kappa_s, line_s, side_s,
    in_sem, send_sem, recv_sem, far_sem, wrap_sem,
):
    b = lax.axis_index("beam")
    c = lax.div(b, 2)
    k = b - 2 * c
    me = lax.axis_index("path")
    g = lax.axis_index("gz")
    nc = nb // 2
    last = nc - 1

    def chip(d, other=False):
        core = (1 - k) if other else k
        return {"beam": (c + d) * 2 + core}

    def ring(axis, at, n):
        return {axis: jnp.where(at >= n, at - n, at)}

    partner = {"beam": c * 2 + (1 - k)}
    b_lo = {"beam": b - 1}
    b_hi = {"beam": b + 1}
    g_lo = ring("gz", g + nz - 1, nz)
    g_hi = ring("gz", g + 1, nz)
    p_to = [ring("path", me + r, np_) for r in (1, 2, 3)]
    p_lo, p_hi = p_to[2], p_to[0]

    barrier = pltpu.get_barrier_semaphore()

    def greet(p):
        pl.semaphore_signal(barrier, 1, device_id=p)

    def both(d, act, cond):
        @pl.when(cond)
        def _():
            act(chip(d))
            act(chip(d, True))

    for d in (3, 2, 1):
        both(-d, greet, c - d >= 0)
        both(d, greet, c + d <= last)
    both(11, greet, (c >= 2) & (c <= 4))
    both(12, greet, (c >= 1) & (c <= 3))
    for p in p_to + [g_lo, g_hi, partner]:
        greet(p)
    wrapped = c >= last - 2
    met = 6 + 2 * (jnp.minimum(c, 3) + jnp.minimum(last - c, 3))
    met = met + jnp.where(wrapped, 4, 0)

    loads = []
    for i, (src, dst) in enumerate(((beta_h, beta_s), (view_h, view_s))):
        cp = pltpu.make_async_copy(src, dst, in_sem.at[E + 1 + i])
        cp.start()
        loads.append(cp)
    tables = loads
    loads = []
    for e in range(E):
        cp = pltpu.make_async_copy(maps_h.at[pl.ds(e * 128, 128)], maps_v.at[pl.ds(e * 128, 128)], in_sem.at[e])
        cp.start()
        loads.append(cp)
    meas_cp = pltpu.make_async_copy(meas_h, meas_v, in_sem.at[E])
    meas_cp.start()
    lines = []
    for i, (src, dst) in enumerate(((kappa_h, kappa_s), (line_h, line_s), (side_h, side_s))):
        cp = pltpu.make_async_copy(src, dst, in_sem.at[E + 3 + i])
        cp.start()
        lines.append(cp)

    @pl.when(c < 1)
    def _():
        sr_v[0] = jnp.zeros((Z, Y), F32)

    @pl.when(c < 2)
    def _():
        sr_v[1] = jnp.zeros((Z, Y), F32)

    @pl.when(c < 3)
    def _():
        vr_v[0] = jnp.zeros((Z, Y), F32)
        vr_v[1] = jnp.zeros((Z, Y), F32)

    @pl.when(c < EARLY + 3)
    def _():
        vr_v[2] = jnp.zeros((Z, Y), F32)
        vr_v[3] = jnp.zeros((Z, Y), F32)

    @pl.when(c < last - 2)
    def _():
        for i in range(4, 8):
            vr_v[i] = jnp.zeros((Z, Y), F32)

    @pl.when(b == 0)
    def _():
        for it in range(2):
            xr_v[it, 0] = jnp.zeros((K, Y), F32)

    @pl.when(b == nb - 1)
    def _():
        for it in range(2):
            xr_v[it, 1] = jnp.zeros((K, Y), F32)

    copies = []

    def send(src, dst, n, to, cond=None):
        cp = pltpu.make_async_remote_copy(src, dst, send_sem.at[n], recv_sem.at[n], device_id=to)
        if cond is None:
            cp.start()
        else:
            pl.when(cond)(cp.start)
        copies.append((cond, cp))
        return cp

    def arrive(cp, cond=None):
        if cond is None:
            cp.wait_recv()
        else:
            pl.when(cond)(cp.wait_recv)

    lane = lax.broadcasted_iota(jnp.int32, (X, Y), 1)
    sub = lax.broadcasted_iota(jnp.int32, (X, Y), 0)
    lane3 = lax.broadcasted_iota(jnp.int32, (Z, X, Y), 2)
    sub3 = lax.broadcasted_iota(jnp.int32, (Z, X, Y), 1)

    def blk(ref, e):
        return ref[pl.ds(e * 128, 128), :].reshape(Z, X, Y)

    def put(ref, e, v3):
        ref[pl.ds(e * 128, 128), :] = v3.reshape(128, Y)

    def compact(e, r3):
        acc = jnp.zeros((X, Y), F32)
        for z in range(Z):
            acc = jnp.where(lane == e * Z + z, r3[z], acc)
        return acc

    def flag(cond):
        return cond.astype(F32)

    for cp in tables:
        cp.wait()
    acc = None
    for e in range(E):
        loads[e].wait()
        t = blk(maps_v, e) * beta_s[view_s[0], e]
        acc = t if acc is None else acc + t
    slab = jnp.sum(acc, axis=1)
    s_v[...] = slab

    inc = acc
    for sh in (1, 2, 4):
        inc = inc + jnp.where(sub3 >= sh, pltpu.roll(inc, sh, 1), 0.0)
    ins_v[...] = (inc - acc).reshape(128, Y) * (1.0 / (nb * X))

    for cp in lines:
        cp.wait()
    rows = jnp.zeros((X, Y), F32)
    for e in range(E):
        rows = rows + compact(e, jnp.sum(blk(maps_v, e), axis=2, keepdims=True))
    strip = jnp.zeros((X, Y), F32)
    for j in range(E):
        mix = jnp.zeros((X, Y), F32)
        for e in range(E):
            mix = jnp.where(lane // Z == e, kappa_s[(e - j) % E, line_s[e]], mix)
        strip = strip + mix * (pltpu.roll(rows, Z * j, 1) if j else rows)
    strip_g[me] = strip

    def compact_faces(ref):
        lo = jnp.zeros((X, Y), F32)
        hi = jnp.zeros((X, Y), F32)
        for e in range(E):
            v = blk(ref, e)
            lo = lo + compact(e, v[:, :, 0:1])
            hi = hi + compact(e, v[:, :, Y - 1 : Y])
        return lo, hi

    def pack_x(ref, it):
        xs_v[it, 0] = ref[pl.ds(0, K, stride=X), :]
        xs_v[it, 1] = ref[pl.ds(X - 1, K, stride=X), :]

    def pack_z(ref, it):
        for e in range(E):
            zs_v[it, 0, pl.ds(e * X, X), :] = ref[pl.ds(e * 128, X), :]
            zs_v[it, 1, pl.ds(e * X, X), :] = ref[pl.ds(e * 128 + 120, X), :]

    def send_x(it):
        return [
            (send(xs_v.at[it, 0], xr_v.at[it, 1], M_H0 + 6 * it + 1, b_lo, b > 0), b < nb - 1),
            (send(xs_v.at[it, 1], xr_v.at[it, 0], M_H0 + 6 * it + 0, b_hi, b < nb - 1), b > 0),
        ]

    def send_z(it):
        return [
            (send(zs_v.at[it, 0], zr_v.at[it, 1], M_H0 + 6 * it + 3, g_lo), None),
            (send(zs_v.at[it, 1], zr_v.at[it, 0], M_H0 + 6 * it + 2, g_hi), None),
        ]

    def send_y(it):
        return [
            (send(ys_v.at[it, 0], yr_v.at[it, 1], M_H0 + 6 * it + 5, p_lo), None),
            (send(ys_v.at[it, 1], yr_v.at[it, 0], M_H0 + 6 * it + 4, p_hi), None),
        ]

    upper = (
        lax.broadcasted_iota(jnp.int32, (Y, Y), 0) < lax.broadcasted_iota(jnp.int32, (Y, Y), 1)
    ).astype(jnp.bfloat16)

    def absorb(e, _):
        mo = None
        for f in range(E):
            t = maps_v[pl.ds(f * 128, 128), :] * kappa_s[f, line_s[e]]
            mo = t if mo is None else mo + t
        fwd = sum(jnp.dot(part, upper, preferred_element_type=F32) for part in split2(mo))
        far = side_s[e].astype(F32)
        pre_v[pl.ds(pl.multiple_of(e * 128, 128), 128), :] = (1.0 - 2.0 * far) * fwd - far * mo
        return 0

    def interior(v3, p0, e):
        def step(diff, p):
            return clip(0.5 * diff) if p is None else clip(blk(p, e) + 0.5 * diff)

        px = jnp.where(sub3 == X - 1, 0.0, step(pltpu.roll(v3, X - 1, 1) - v3, p0 and p0[0]))
        py = jnp.where(lane3 == Y - 1, 0.0, step(pltpu.roll(v3, Y - 1, 2) - v3, p0 and p0[1]))
        zero = jnp.zeros((1, X, Y), F32)
        diff = jnp.concatenate([v3[1:] - v3[:-1], zero], axis=0)
        pz = step(diff, p0 and p0[2])
        adj = (pltpu.roll(px, 1, 1) - px) + (pltpu.roll(py, 1, 2) - py)
        adj = adj + (jnp.concatenate([zero, pz[:-1]], axis=0) - jnp.concatenate([pz[:-1], zero], axis=0))
        return adj, px, py, pz

    def first_dual(e, _):
        e = pl.multiple_of(e * 128, 128) // 128
        adj, px, py, pz = interior(blk(maps_v, e), None, e)
        put(adj_v, e, adj)
        put(px_v, e, px)
        put(py_v, e, py)
        put(pz_v, e, pz)
        return 0

    def alone():
        lax.fori_loop(0, E, absorb, 0)
        pack_x(maps_v, 0)
        pack_z(maps_v, 0)
        lo, hi = compact_faces(maps_v)
        ys_v[0, 0] = lo
        ys_v[0, 1] = hi
        lax.fori_loop(0, E, first_dual, 0)

    waits = (c >= 1) & (c < EARLY)
    pl.when(waits)(alone)
    pl.semaphore_wait(barrier, met)

    def tell(sem):
        return lambda p: pl.semaphore_signal(sem, 1, device_id=p)

    def windows(src, at, d, cond):
        return [send(v_v.at[src], vr_v.at[at + o], M_V + at + o, chip(d, o == 1), cond) for o in range(2)]

    s_cp = [send(s_v, sr_v.at[i], M_S + i, chip(i + 1), c + i + 1 <= last) for i in (1, 0)]
    s_cp.reverse()
    strip_cp = [send(strip_g.at[me], strip_g.at[me], M_STRIP + i, p_to[i]) for i in (1, 0, 2)]

    @pl.when(c == 0)
    def _():
        v_v[1] = s_v[...]

    windows(1, 0, 3, c == 0)
    both(-3, tell(far_sem), (c >= EARLY) & (c <= last - 3))
    both(-11, tell(wrap_sem), wrapped)
    both(-12, tell(wrap_sem), wrapped)
    back = [send(s_v, bk_v.at[i], M_BACK + i, chip(-i - 1), (c >= 3 + i) & (c <= 5 + i)) for i in range(2)]
    pl.when(~waits)(alone)
    my0, my1 = ys_v[0, 0], ys_v[0, 1]

    for i in range(2):
        arrive(s_cp[i], c >= i + 1)
    near = sr_v[0] + sr_v[1]
    v_v[0] = s_v[...] + near

    three = windows(0, 0, 3, (c >= EARLY) & (c <= last - 3))
    m_v[...] = near + s_v[...] * flag(k == 0)
    m_cp = send(m_v, mr_v, M_CORE, partner)
    h0 = send_x(0) + send_z(0) + send_y(0)

    @pl.when((c >= EARLY - 1) & (c <= last - 6))
    def _():
        pl.semaphore_wait(far_sem, 2)

    six = windows(0, 2, 6, (c >= EARLY - 1) & (c <= last - 6))

    @pl.when(waits)
    def _():
        pl.when(c >= 3)(three[0].wait_recv)
        v_v[1] = v_v[0] + vr_v[0]

    windows(1, 0, 3, waits)

    @pl.when((c >= EARLY - 3) & (c < EARLY - 1))
    def _():
        pl.semaphore_wait(far_sem, 2)

    windows(1, 2, 6, (c >= EARLY - 3) & (c < EARLY - 1))

    for cp in strip_cp:
        cp.wait_recv()
    side_row = jnp.zeros((X, Y), F32)
    for e in range(E):
        side_row = jnp.where(lane // Z == e, side_s[e].astype(F32), side_row)
    below = jnp.zeros((X, Y), F32)
    above = jnp.zeros((X, Y), F32)
    for r in range(4):
        below = below + strip_g[r] * flag(me > r)
        above = above + strip_g[r] * flag(me <= r)
    offset = jnp.where(side_row == 0.0, below, above)
    ny = np_ * Y
    for e in range(E):
        local = blk(pre_v, e)
        ins = ins_v[...].reshape(Z, X, Y)
        parts = []
        for z in range(Z):
            n = e * Z + z
            parts.append(jnp.exp(-(offset[:, n : n + 1] + local[z]) * (1.0 / ny) - ins[z]))
        put(pre_v, e, jnp.stack(parts))

    m_xlo, m_xhi = flag(b > 0), flag(b < nb - 1)
    m_zlo, m_zhi = flag(g > 0), flag(g < nz - 1)
    m_ylo, m_yhi = flag(me > 0), flag(me < np_ - 1)
    ymask = flag(lane == 0) - flag(lane == Y - 1)
    xmask = flag(sub == 0) - flag(sub == X - 1)

    def faces(it, hs, q):
        for cp, cond in hs:
            arrive(cp, cond)
        qx = (
            clip(q[0] + (0.5 * m_xlo) * (xs_v[it, 0] - xr_v[it, 0])),
            clip(q[1] + (0.5 * m_xhi) * (xr_v[it, 1] - xs_v[it, 1])),
        )
        qz = (
            clip(q[2] + (0.5 * m_zlo) * (zs_v[it, 0] - zr_v[it, 0])),
            clip(q[3] + (0.5 * m_zhi) * (zr_v[it, 1] - zs_v[it, 1])),
        )
        qy = (
            clip(q[4] + (0.5 * m_ylo) * (ys_v[it, 0] - yr_v[it, 0])),
            clip(q[5] + (0.5 * m_yhi) * (yr_v[it, 1] - ys_v[it, 1])),
        )
        return qx + qz + qy

    def boundary(e, q):
        shifted = pltpu.roll(q[5], Y - 1, 1)
        even = lax.rem(lane, 2) == 0
        pair = (jnp.where(even, q[4], shifted), jnp.where(even, shifted, q[4]))
        parts = []
        for z in range(Z):
            n = e * Z + z
            r = pair[n % 2]
            if n:
                r = pltpu.roll(r, Y - n, 1)
            lo = jnp.broadcast_to(qx_v[0, pl.ds(n, 1), :], (X, Y))
            hi = jnp.broadcast_to(qx_v[1, pl.ds(n, 1), :], (X, Y))
            t = r * ymask + jnp.where(sub == 0, lo, hi) * xmask
            if z == 0:
                t = t + q[2][e * X : (e + 1) * X]
            if z == Z - 1:
                t = t - q[3][e * X : (e + 1) * X]
            parts.append(t)
        return jnp.stack(parts)

    q0 = faces(0, h0, (0.0,) * 6)
    qx_v[0] = q0[0]
    qx_v[1] = q0[1]
    for e in range(E):
        put(adj_v, e, blk(adj_v, e) + boundary(e, q0))
    qz0 = (q0[2], q0[3])
    qy0 = (q0[4], q0[5])
    zs_v[2, 0] = qz0[0]
    zs_v[2, 1] = qz0[1]

    meas_cp.wait()
    meas = jnp.zeros((X, Y), F32)
    for e in range(E):
        row = jnp.pad(meas_v[pl.ds(e * X, X), :], ((0, 0), (0, Y - Z)))
        meas = meas + (pltpu.roll(row, e * Z, 1) if e else row)

    arrive(m_cp)
    arrive(three[0], c >= EARLY)
    arrive(three[1], c >= 3)
    for cp in six:
        arrive(cp, c >= EARLY + 3)

    for i in range(4, 8):
        cp = pltpu.make_async_remote_copy(
            v_v.at[2], vr_v.at[i], send_sem.at[M_V + i], recv_sem.at[M_V + i], device_id=partner
        )
        arrive(cp, wrapped)
    carry = (sr_v[0] + sr_v[1] + mr_v[...]) + (vr_v[0] + vr_v[1]) + (vr_v[2] + vr_v[3])
    carry = carry + ((vr_v[4] + vr_v[5]) + (vr_v[6] + vr_v[7]))
    att_v[...] = jnp.exp(carry * (-1.0 / (nb * X)))
    projs = jnp.zeros((X, Y), F32)
    totals = jnp.zeros((X, Y), F32)
    attb = jnp.stack([jnp.broadcast_to(att_v[pl.ds(z, 1), :], (X, Y)) for z in range(Z)])
    for e in range(E):
        w = blk(pre_v, e) * attb
        put(w_v, e, w)
        totals = totals + compact(e, jnp.sum(w, axis=2, keepdims=True))
        projs = projs + compact(e, jnp.sum(w * blk(maps_v, e), axis=2, keepdims=True))
    b_g[me, 0] = projs
    b_g[me, 1] = totals
    b_cp = [send(b_g.at[me], b_g.at[me], M_B + i, p_to[i]) for i in (1, 0, 2)]

    span = (c >= 2) & (c <= 4)
    whole = (c >= 1) & (c <= 3)

    @pl.when(span)
    def _():
        for cp in back:
            cp.wait_recv()
        v_v[2] = s_v[...] + bk_v[0] + bk_v[1]

    def wrap_sends():
        @pl.when(span | whole)
        def _():
            pl.semaphore_wait(wrap_sem, 2 * (span.astype(jnp.int32) + whole.astype(jnp.int32)))

        return windows(2, 4, 11, span) + windows(1, 6, 12, whole)

    wrap_sends()

    by0 = jnp.zeros((X, Y), F32)
    by1 = jnp.zeros((X, Y), F32)
    ty0 = jnp.zeros((X, Y), F32)
    ty1 = jnp.zeros((X, Y), F32)
    for e in range(E):
        w = blk(w_v, e)
        tau = 1.0 / (w + 6.0)
        tw = tau * w
        base = blk(maps_v, e) - tau * blk(adj_v, e)
        put(tau_v, e, tau)
        put(tw_v, e, tw)
        put(base_v, e, base)
        by0 = by0 + compact(e, base[:, :, 0:1])
        by1 = by1 + compact(e, base[:, :, Y - 1 : Y])
        ty0 = ty0 + compact(e, tw[:, :, 0:1])
        ty1 = ty1 + compact(e, tw[:, :, Y - 1 : Y])

    for cp in b_cp:
        cp.wait_recv()
    total = (b_g[0] + b_g[1]) + (b_g[2] + b_g[3])
    proj = total[0]
    sig = 1.0 / total[1]
    inv = 1.0 / (1.0 + sig)
    dd = sig * (proj - meas) * inv

    ey0 = 2.0 * jnp.maximum(by0 - ty0 * dd, 0.0) - ys_v[0, 0]
    ey1 = 2.0 * jnp.maximum(by1 - ty1 * dd, 0.0) - ys_v[0, 1]
    ys_v[1, 0] = ey0
    ys_v[1, 1] = ey1
    h1 = send_y(1)

    def spread(vec, e):
        return jnp.stack(
            [jnp.broadcast_to(vec[:, n : n + 1], (X, Y)) for n in range(e * Z, (e + 1) * Z)]
        )

    image = jnp.zeros((X, Y), F32)
    for e in range(E):
        u = jnp.maximum(blk(base_v, e) - blk(tw_v, e) * spread(dd, e), 0.0)
        ext = 2.0 * u - blk(maps_v, e)
        put(u_v, e, u)
        put(ext_v, e, ext)
        image = image + compact(e, jnp.sum(blk(w_v, e) * ext, axis=2, keepdims=True))
    c_g[me] = image
    c_cp = [send(c_g.at[me], c_g.at[me], M_C + i, p_to[i]) for i in (1, 0, 2)]
    pack_x(ext_v, 1)
    h1 += send_x(1)
    pack_z(ext_v, 1)
    h1 += send_z(1)

    def rows_out(ref, v):
        for e in range(E):
            turned = pltpu.roll(v, Y - e * Z, 1) if e else v
            ref[pl.ds(e * X, X), :] = turned[:, :Z]

    rows_out(emis_o, proj * (1.0 / ny))

    for e in range(E):
        adj, _, _, _ = interior(blk(ext_v, e), (px_v, py_v, pz_v), e)
        put(base_v, e, blk(u_v, e) - blk(tau_v, e) * adj)

    q1 = faces(1, h1, (qx_v[0], qx_v[1], zs_v[2, 0], zs_v[2, 1]) + qy0)
    qx_v[0] = q1[0]
    qx_v[1] = q1[1]
    for e in range(E):
        put(base_v, e, blk(base_v, e) - blk(tau_v, e) * boundary(e, q1))

    for cp in c_cp:
        cp.wait_recv()
    image = (c_g[0] + c_g[1]) + (c_g[2] + c_g[3])
    dd = (dd + sig * (image - meas)) * inv
    for e in range(E):
        put(out_o, e, jnp.maximum(blk(base_v, e) - blk(tw_v, e) * spread(dd, e), 0.0))
    rows_out(dd_o, dd)
    for cond, cp in copies:
        if cond is None:
            cp.wait_send()
        else:
            pl.when(cond)(cp.wait_send)


def flush(a_ref, b_ref, c_ref, a_o, b_o, c_o, sem):
    parts = [(b_ref.at[pl.ds(i * 256, 256)], b_o.at[pl.ds(i * 256, 256)]) for i in range(4)]
    parts += [(a_ref, a_o), (c_ref, c_o)]
    copies = [pltpu.make_async_copy(src, dst, sem.at[i]) for i, (src, dst) in enumerate(parts)]
    for cp in copies:
        cp.start()
    for cp in copies:
        cp.wait()


def shards(maps, measured, beta_table, view, kappa, line_of, side):
    sizes = tuple(lax.axis_size(a) for a in ("beam", "path", "gz"))
    big = pltpu.VMEM((ROWS, Y), F32)
    scratch = [big] * 12 + [
        pltpu.VMEM((128, Y), F32),
        pltpu.VMEM((E * X, Z), F32),
        pltpu.VMEM((Z, Y), F32),
        pltpu.VMEM((2, Z, Y), F32),
        pltpu.VMEM((Z, Y), F32),
        pltpu.VMEM((Z, Y), F32),
        pltpu.VMEM((3, Z, Y), F32),
        pltpu.VMEM((8, Z, Y), F32),
        pltpu.VMEM((2, Z, Y), F32),
        pltpu.VMEM((Z, Y), F32),
        pltpu.VMEM((2, 2, K, Y), F32),
        pltpu.VMEM((2, 2, K, Y), F32),
        pltpu.VMEM((3, 2, E * X, Y), F32),
        pltpu.VMEM((2, 2, E * X, Y), F32),
        pltpu.VMEM((2, 2, X, Y), F32),
        pltpu.VMEM((2, 2, X, Y), F32),
        pltpu.VMEM((2, K, Y), F32),
        pltpu.VMEM((4, X, Y), F32),
        pltpu.VMEM((4, 2, X, Y), F32),
        pltpu.VMEM((4, X, Y), F32),
        pltpu.SMEM(beta_table.shape, F32),
        pltpu.SMEM(view.shape, jnp.int32),
        pltpu.SMEM(kappa.shape[::-1], F32),
        pltpu.SMEM(line_of.shape, jnp.int32),
        pltpu.SMEM(side.shape, jnp.int32),
        pltpu.SemaphoreType.DMA((E + 6,)),
        pltpu.SemaphoreType.DMA((M_N,)),
        pltpu.SemaphoreType.DMA((M_N,)),
        pltpu.SemaphoreType.REGULAR,
        pltpu.SemaphoreType.REGULAR,
    ]
    emission, out, dual = pl.pallas_call(
        functools.partial(kernel, *sizes),
        out_shape=(
            pltpu.VMEM((E * X, Z), F32),
            pltpu.VMEM((ROWS, Y), F32),
            pltpu.VMEM((E * X, Z), F32),
        ),
        in_specs=[pl.BlockSpec(memory_space=pltpu.HBM)] * 7,
        scratch_shapes=scratch,
        compiler_params=pltpu.CompilerParams(collective_id=0, has_side_effects=True),
        name="xrf",
    )(
        maps.reshape(ROWS, Y),
        measured.transpose(0, 2, 1).reshape(E * X, Z),
        beta_table,
        view,
        kappa.T,
        line_of,
        side,
    )
    hbm = pl.BlockSpec(memory_space=pltpu.HBM)
    vmem = pl.BlockSpec(memory_space=pltpu.VMEM)
    emission, out, dual = pl.pallas_call(
        flush,
        out_shape=tuple(jax.ShapeDtypeStruct(a.shape, F32) for a in (emission, out, dual)),
        in_specs=[vmem] * 3,
        out_specs=(hbm,) * 3,
        scratch_shapes=[pltpu.SemaphoreType.DMA((6,))],
        name="flush",
    )(*(pltpu.with_memory_space_constraint(a, pltpu.VMEM) for a in (emission, out, dual)))
    return (
        emission.reshape(E, X, Z).transpose(0, 2, 1),
        out.reshape(E, Z, X, Y),
        dual.reshape(E, X, Z).transpose(0, 2, 1),
    )


def solution(mesh):
    return jax.shard_map(
        shards,
        mesh=mesh,
        in_specs=(P(None, "gz", "beam", "path"), P(None, "gz", "beam"), P(), P(), P(), P(), P()),
        out_specs=(P(None, "gz", "beam"), P(None, "gz", "beam", "path"), P(None, "gz", "beam")),
        check_vma=False,
    )
```

```python
import functools

import jax
import jax.numpy as jnp
from jax import lax
from jax.experimental import pallas as pl
from jax.experimental.pallas import tpu as pltpu
from jax.sharding import PartitionSpec as P

LAM = 0.1
F32 = jnp.float32
E, Z, X, Y = 8, 16, 8, 128
K = E * Z
ROWS = K * X

M_S = 0
M_CORE = 2
M_V = 3
M_H0 = 11
M_H1 = 17
M_STRIP = 23
M_B = 26
M_C = 29
M_BACK = 32
M_X = 34
M_N = 36
EARLY = 8


def clip(v):
    return jnp.clip(v, -LAM, LAM)


def split2(v):
    hi = v.astype(jnp.bfloat16)
    rest = v - hi.astype(F32)
    mid = rest.astype(jnp.bfloat16)
    return hi, mid


def kernel(
    nb, np_, nz,
    maps_h, meas_h, beta_h, view_h, kappa_h, line_h, side_h,
    emis_o, out_o, dd_o,
    maps_v, w_v, pre_v, px_v, py_v, pz_v, adj_v, tau_v, tw_v, base_v, u_v, ext_v, ins_v, meas_v,
    s_v, sr_v, m_v, mr_v, v_v, vr_v, bk_v, att_v,
    xs_v, xr_v, zs_v, zr_v, ys_v, yr_v, qx_v,
    strip_g, b_g, c_g,
    beta_s, view_s, kappa_s, line_s, side_s,
    in_sem, send_sem, recv_sem, far_sem, wrap_sem,
):
    b = lax.axis_index("beam")
    c = lax.div(b, 2)
    k = b - 2 * c
    me = lax.axis_index("path")
    g = lax.axis_index("gz")
    nc = nb // 2
    last = nc - 1

    def chip(d, other=False):
        core = (1 - k) if other else k
        return {"beam": (c + d) * 2 + core}

    def ring(axis, at, n):
        return {axis: jnp.where(at >= n, at - n, at)}

    partner = {"beam": c * 2 + (1 - k)}
    b_lo = {"beam": b - 1}
    b_hi = {"beam": b + 1}
    g_lo = ring("gz", g + nz - 1, nz)
    g_hi = ring("gz", g + 1, nz)
    p_to = [ring("path", me + r, np_) for r in (1, 2, 3)]
    p_lo, p_hi = p_to[2], p_to[0]

    barrier = pltpu.get_barrier_semaphore()

    def greet(p):
        pl.semaphore_signal(barrier, 1, device_id=p)

    def both(d, act, cond):
        @pl.when(cond)
        def _():
            act(chip(d))
            act(chip(d, True))

    for d in (3, 2, 1):
        both(-d, greet, c - d >= 0)
        both(d, greet, c + d <= last)
    both(11, greet, (c >= 2) & (c <= 4))
    both(12, greet, (c >= 1) & (c <= 3))
    for p in p_to + [g_lo, g_hi, partner]:
        greet(p)
    wrapped = c >= last - 2
    met = 6 + 2 * (jnp.minimum(c, 3) + jnp.minimum(last - c, 3))
    met = met + jnp.where(wrapped, 4, 0)

    loads = []
    for i, (src, dst) in enumerate(((beta_h, beta_s), (view_h, view_s))):
        cp = pltpu.make_async_copy(src, dst, in_sem.at[E + 1 + i])
        cp.start()
        loads.append(cp)
    tables = loads
    loads = []
    for e in range(E):
        cp = pltpu.make_async_copy(maps_h.at[pl.ds(e * 128, 128)], maps_v.at[pl.ds(e * 128, 128)], in_sem.at[e])
        cp.start()
        loads.append(cp)
    meas_cp = pltpu.make_async_copy(meas_h, meas_v, in_sem.at[E])
    meas_cp.start()
    lines = []
    for i, (src, dst) in enumerate(((kappa_h, kappa_s), (line_h, line_s), (side_h, side_s))):
        cp = pltpu.make_async_copy(src, dst, in_sem.at[E + 3 + i])
        cp.start()
        lines.append(cp)

    @pl.when(c < 1)
    def _():
        sr_v[0] = jnp.zeros((Z, Y), F32)

    @pl.when(c < 2)
    def _():
        sr_v[1] = jnp.zeros((Z, Y), F32)

    @pl.when(c < 3)
    def _():
        vr_v[0] = jnp.zeros((Z, Y), F32)
        vr_v[1] = jnp.zeros((Z, Y), F32)

    @pl.when(c < EARLY + 3)
    def _():
        vr_v[2] = jnp.zeros((Z, Y), F32)
        vr_v[3] = jnp.zeros((Z, Y), F32)

    @pl.when(c < last - 2)
    def _():
        for i in range(4, 8):
            vr_v[i] = jnp.zeros((Z, Y), F32)

    @pl.when(b == 0)
    def _():
        for it in range(2):
            xr_v[it, 0] = jnp.zeros((K, Y), F32)

    @pl.when(b == nb - 1)
    def _():
        for it in range(2):
            xr_v[it, 1] = jnp.zeros((K, Y), F32)

    copies = []

    def send(src, dst, n, to, cond=None):
        cp = pltpu.make_async_remote_copy(src, dst, send_sem.at[n], recv_sem.at[n], device_id=to)
        if cond is None:
            cp.start()
        else:
            pl.when(cond)(cp.start)
        copies.append((cond, cp))
        return cp

    def drain(some):
        for cond, cp in some:
            if cond is None:
                cp.wait_send()
            else:
                pl.when(cond)(cp.wait_send)

    def arrive(cp, cond=None):
        if cond is None:
            cp.wait_recv()
        else:
            pl.when(cond)(cp.wait_recv)

    lane = lax.broadcasted_iota(jnp.int32, (X, Y), 1)
    sub = lax.broadcasted_iota(jnp.int32, (X, Y), 0)
    lane3 = lax.broadcasted_iota(jnp.int32, (Z, X, Y), 2)
    sub3 = lax.broadcasted_iota(jnp.int32, (Z, X, Y), 1)

    def blk(ref, e):
        return ref[pl.ds(e * 128, 128), :].reshape(Z, X, Y)

    def put(ref, e, v3):
        ref[pl.ds(e * 128, 128), :] = v3.reshape(128, Y)

    def compact(e, r3):
        acc = jnp.zeros((X, Y), F32)
        for z in range(Z):
            acc = jnp.where(lane == e * Z + z, r3[z], acc)
        return acc

    def flag(cond):
        return cond.astype(F32)

    ones = jnp.ones((Y, Y), jnp.bfloat16)
    square = (128, Y)
    chosen = lax.broadcasted_iota(jnp.int32, square, 1) == lax.broadcasted_iota(jnp.int32, square, 0) // X

    def times_ones(parts):
        return sum(jnp.dot(p, ones, preferred_element_type=F32) for p in parts)

    def row_sums(e, v3):
        return compact(e, times_ones(split2(v3.reshape(128, Y))).reshape(Z, X, Y))

    for cp in tables:
        cp.wait()
    acc = None
    for e in range(E):
        loads[e].wait()
        t = blk(maps_v, e) * beta_s[view_s[0], e]
        acc = t if acc is None else acc + t
    slab = jnp.sum(acc, axis=1)
    s_v[...] = slab

    inc = acc
    for sh in (1, 2, 4):
        inc = inc + jnp.where(sub3 >= sh, pltpu.roll(inc, sh, 1), 0.0)
    ins_v[...] = (inc - acc).reshape(128, Y) * (1.0 / (nb * X))

    for cp in lines:
        cp.wait()
    rows = jnp.zeros((X, Y), F32)
    for e in range(E):
        rows = rows + compact(e, jnp.sum(blk(maps_v, e), axis=2, keepdims=True))
    strip = jnp.zeros((X, Y), F32)
    for j in range(E):
        mix = jnp.zeros((X, Y), F32)
        for e in range(E):
            mix = jnp.where(lane // Z == e, kappa_s[(e - j) % E, line_s[e]], mix)
        strip = strip + mix * (pltpu.roll(rows, Z * j, 1) if j else rows)
    strip_g[me] = strip

    def compact_faces(ref):
        lo = jnp.zeros((X, Y), F32)
        hi = jnp.zeros((X, Y), F32)
        for e in range(E):
            v = blk(ref, e)
            lo = lo + compact(e, v[:, :, 0:1])
            hi = hi + compact(e, v[:, :, Y - 1 : Y])
        return lo, hi

    def pack_x(ref, it):
        xs_v[it, 0] = ref[pl.ds(0, K, stride=X), :]
        xs_v[it, 1] = ref[pl.ds(X - 1, K, stride=X), :]

    def pack_z(ref, it):
        for e in range(E):
            zs_v[it, 0, pl.ds(e * X, X), :] = ref[pl.ds(e * 128, X), :]
            zs_v[it, 1, pl.ds(e * X, X), :] = ref[pl.ds(e * 128 + 120, X), :]

    def send_x(it):
        return [
            (send(xs_v.at[it, 0], xr_v.at[it, 1], M_H0 + 6 * it + 1, b_lo, b > 0), b < nb - 1),
            (send(xs_v.at[it, 1], xr_v.at[it, 0], M_H0 + 6 * it + 0, b_hi, b < nb - 1), b > 0),
        ]

    def send_z(it):
        return [
            (send(zs_v.at[it, 0], zr_v.at[it, 1], M_H0 + 6 * it + 3, g_lo), None),
            (send(zs_v.at[it, 1], zr_v.at[it, 0], M_H0 + 6 * it + 2, g_hi), None),
        ]

    def send_y(it):
        return [
            (send(ys_v.at[it, 0], yr_v.at[it, 1], M_H0 + 6 * it + 5, p_lo), None),
            (send(ys_v.at[it, 1], yr_v.at[it, 0], M_H0 + 6 * it + 4, p_hi), None),
        ]

    upper = (
        lax.broadcasted_iota(jnp.int32, (Y, Y), 0) < lax.broadcasted_iota(jnp.int32, (Y, Y), 1)
    ).astype(jnp.bfloat16)

    def absorb(e, _):
        mo = None
        for f in range(E):
            t = maps_v[pl.ds(f * 128, 128), :] * kappa_s[f, line_s[e]]
            mo = t if mo is None else mo + t
        fwd = sum(jnp.dot(part, upper, preferred_element_type=F32) for part in split2(mo))
        far = side_s[e].astype(F32)
        pre_v[pl.ds(pl.multiple_of(e * 128, 128), 128), :] = (1.0 - 2.0 * far) * fwd - far * mo
        return 0

    def interior(v3, p0, e):
        def step(diff, p):
            return clip(0.5 * diff) if p is None else clip(blk(p, e) + 0.5 * diff)

        px = jnp.where(sub3 == X - 1, 0.0, step(pltpu.roll(v3, X - 1, 1) - v3, p0 and p0[0]))
        py = jnp.where(lane3 == Y - 1, 0.0, step(pltpu.roll(v3, Y - 1, 2) - v3, p0 and p0[1]))
        zero = jnp.zeros((1, X, Y), F32)
        diff = jnp.concatenate([v3[1:] - v3[:-1], zero], axis=0)
        pz = step(diff, p0 and p0[2])
        adj = (pltpu.roll(px, 1, 1) - px) + (pltpu.roll(py, 1, 2) - py)
        adj = adj + (jnp.concatenate([zero, pz[:-1]], axis=0) - jnp.concatenate([pz[:-1], zero], axis=0))
        return adj, px, py, pz

    def first_dual(e, _):
        e = pl.multiple_of(e * 128, 128) // 128
        adj, px, py, pz = interior(blk(maps_v, e), None, e)
        put(adj_v, e, adj)
        put(px_v, e, px)
        put(py_v, e, py)
        put(pz_v, e, pz)
        return 0

    def alone():
        lax.fori_loop(0, E, absorb, 0)
        pack_x(maps_v, 0)
        pack_z(maps_v, 0)
        lo, hi = compact_faces(maps_v)
        ys_v[0, 0] = lo
        ys_v[0, 1] = hi
        lax.fori_loop(0, E, first_dual, 0)

    waits = (c >= 1) & (c < EARLY)
    pl.when(waits)(alone)
    pl.semaphore_wait(barrier, met)

    def tell(sem):
        return lambda p: pl.semaphore_signal(sem, 1, device_id=p)

    def windows(src, at, d, cond):
        return [send(v_v.at[src], vr_v.at[at + o], M_V + at + o, chip(d, o == 1), cond) for o in range(2)]

    s_cp = [send(s_v, sr_v.at[i], M_S + i, chip(i + 1), c + i + 1 <= last) for i in (1, 0)]
    s_cp.reverse()
    strip_cp = [send(strip_g.at[me], strip_g.at[me], M_STRIP + i, p_to[i]) for i in (1, 0, 2)]

    @pl.when(c == 0)
    def _():
        v_v[1] = s_v[...]

    windows(1, 0, 3, c == 0)
    both(-3, tell(far_sem), (c >= EARLY) & (c <= last - 3))
    both(-11, tell(wrap_sem), wrapped)
    both(-12, tell(wrap_sem), wrapped)
    back = [send(s_v, bk_v.at[i], M_BACK + i, chip(-i - 1), (c >= 3 + i) & (c <= 5 + i)) for i in range(2)]
    pl.when(~waits)(alone)
    my0, my1 = ys_v[0, 0], ys_v[0, 1]

    for i in range(2):
        arrive(s_cp[i], c >= i + 1)
    near = sr_v[0] + sr_v[1]
    v_v[0] = s_v[...] + near

    three = windows(0, 0, 3, (c >= EARLY) & (c <= last - 3))
    m_v[...] = near + s_v[...] * flag(k == 0)
    m_cp = send(m_v, mr_v, M_CORE, partner)
    h0 = send_x(0) + send_z(0) + send_y(0)

    @pl.when((c >= EARLY - 1) & (c <= last - 6))
    def _():
        pl.semaphore_wait(far_sem, 2)

    six = windows(0, 2, 6, (c >= EARLY - 1) & (c <= last - 6))

    @pl.when(waits)
    def _():
        pl.when(c >= 3)(three[0].wait_recv)
        v_v[1] = v_v[0] + vr_v[0]

    windows(1, 0, 3, waits)

    @pl.when((c >= EARLY - 3) & (c < EARLY - 1))
    def _():
        pl.semaphore_wait(far_sem, 2)

    windows(1, 2, 6, (c >= EARLY - 3) & (c < EARLY - 1))

    for cp in strip_cp:
        cp.wait_recv()
    side_row = jnp.zeros((X, Y), F32)
    for e in range(E):
        side_row = jnp.where(lane // Z == e, side_s[e].astype(F32), side_row)
    below = jnp.zeros((X, Y), F32)
    above = jnp.zeros((X, Y), F32)
    for r in range(4):
        below = below + strip_g[r] * flag(me > r)
        above = above + strip_g[r] * flag(me <= r)
    offset = jnp.where(side_row == 0.0, below, above)
    ny = np_ * Y
    for e in range(E):
        local = blk(pre_v, e)
        ins = ins_v[...].reshape(Z, X, Y)
        parts = []
        for z in range(Z):
            n = e * Z + z
            parts.append(jnp.exp(-(offset[:, n : n + 1] + local[z]) * (1.0 / ny) - ins[z]))
        put(pre_v, e, jnp.stack(parts))

    m_xlo, m_xhi = flag(b > 0), flag(b < nb - 1)
    m_zlo, m_zhi = flag(g > 0), flag(g < nz - 1)
    m_ylo, m_yhi = flag(me > 0), flag(me < np_ - 1)
    ymask = flag(lane == 0) - flag(lane == Y - 1)
    xmask = flag(sub == 0) - flag(sub == X - 1)

    def faces(it, hs, q):
        for cp, cond in hs:
            arrive(cp, cond)
        qx = (
            clip(q[0] + (0.5 * m_xlo) * (xs_v[it, 0] - xr_v[it, 0])),
            clip(q[1] + (0.5 * m_xhi) * (xr_v[it, 1] - xs_v[it, 1])),
        )
        qz = (
            clip(q[2] + (0.5 * m_zlo) * (zs_v[it, 0] - zr_v[it, 0])),
            clip(q[3] + (0.5 * m_zhi) * (zr_v[it, 1] - zs_v[it, 1])),
        )
        qy = (
            clip(q[4] + (0.5 * m_ylo) * (ys_v[it, 0] - yr_v[it, 0])),
            clip(q[5] + (0.5 * m_yhi) * (yr_v[it, 1] - ys_v[it, 1])),
        )
        return qx + qz + qy

    def boundary(e, q):
        shifted = pltpu.roll(q[5], Y - 1, 1)
        even = lax.rem(lane, 2) == 0
        pair = (jnp.where(even, q[4], shifted), jnp.where(even, shifted, q[4]))
        parts = []
        for z in range(Z):
            n = e * Z + z
            r = pair[n % 2]
            if n:
                r = pltpu.roll(r, Y - n, 1)
            lo = jnp.broadcast_to(qx_v[0, pl.ds(n, 1), :], (X, Y))
            hi = jnp.broadcast_to(qx_v[1, pl.ds(n, 1), :], (X, Y))
            t = r * ymask + jnp.where(sub == 0, lo, hi) * xmask
            if z == 0:
                t = t + q[2][e * X : (e + 1) * X]
            if z == Z - 1:
                t = t - q[3][e * X : (e + 1) * X]
            parts.append(t)
        return jnp.stack(parts)

    q0 = faces(0, h0, (0.0,) * 6)
    qx_v[0] = q0[0]
    qx_v[1] = q0[1]
    for e in range(E):
        put(adj_v, e, blk(adj_v, e) + boundary(e, q0))
    qz0 = (q0[2], q0[3])
    qy0 = (q0[4], q0[5])
    zs_v[2, 0] = qz0[0]
    zs_v[2, 1] = qz0[1]

    meas_cp.wait()
    meas = jnp.zeros((X, Y), F32)
    for e in range(E):
        row = jnp.pad(meas_v[pl.ds(e * X, X), :], ((0, 0), (0, Y - Z)))
        meas = meas + (pltpu.roll(row, e * Z, 1) if e else row)

    span = (c >= 2) & (c <= 4)
    whole = (c >= 1) & (c <= 3)

    @pl.when(span)
    def _():
        for cp in back:
            cp.wait_recv()
        v_v[2] = s_v[...] + bk_v[0] + bk_v[1]

    def wrap_sends(at):
        @pl.when(at & (span | whole))
        def _():
            pl.semaphore_wait(wrap_sem, 2 * (span.astype(jnp.int32) + whole.astype(jnp.int32)))

        windows(2, 4, 11, at & span)
        windows(1, 6, 12, at & whole)

    wrap_sends(c >= 3)

    arrive(m_cp)
    arrive(three[0], c >= EARLY)
    arrive(three[1], c >= 3)
    for cp in six:
        arrive(cp, c >= EARLY + 3)

    for i in range(4, 8):
        cp = pltpu.make_async_remote_copy(
            v_v.at[2], vr_v.at[i], send_sem.at[M_V + i], recv_sem.at[M_V + i], device_id=partner
        )
        arrive(cp, wrapped)
    carry = (sr_v[0] + sr_v[1] + mr_v[...]) + (vr_v[0] + vr_v[1]) + (vr_v[2] + vr_v[3])
    carry = carry + ((vr_v[4] + vr_v[5]) + (vr_v[6] + vr_v[7]))
    att_v[...] = jnp.exp(carry * (-1.0 / (nb * X)))
    projs = jnp.zeros((X, Y), F32)
    totals = jnp.zeros((X, Y), F32)
    attb = jnp.stack([jnp.broadcast_to(att_v[pl.ds(z, 1), :], (X, Y)) for z in range(Z)])
    for e in range(E):
        w = blk(pre_v, e) * attb
        put(w_v, e, w)
        totals = totals + row_sums(e, w)
        projs = projs + compact(e, jnp.sum(w * blk(maps_v, e), axis=2, keepdims=True))
    b_g[me, 0] = projs
    b_g[me, 1] = totals
    b_cp = [send(b_g.at[me], b_g.at[me], M_B + i, p_to[i]) for i in (1, 0, 2)]

    wrap_sends(c < 3)

    by0 = jnp.zeros((X, Y), F32)
    by1 = jnp.zeros((X, Y), F32)
    ty0 = jnp.zeros((X, Y), F32)
    ty1 = jnp.zeros((X, Y), F32)
    for e in range(E):
        w = blk(w_v, e)
        tau = 1.0 / (w + 6.0)
        tw = tau * w
        base = blk(maps_v, e) - tau * blk(adj_v, e)
        put(tau_v, e, tau)
        put(tw_v, e, tw)
        put(base_v, e, base)
        by0 = by0 + compact(e, base[:, :, 0:1])
        by1 = by1 + compact(e, base[:, :, Y - 1 : Y])
        ty0 = ty0 + compact(e, tw[:, :, 0:1])
        ty1 = ty1 + compact(e, tw[:, :, Y - 1 : Y])

    for cp in b_cp:
        cp.wait_recv()
    total = (b_g[0] + b_g[1]) + (b_g[2] + b_g[3])
    proj = total[0]
    sig = 1.0 / total[1]
    inv = 1.0 / (1.0 + sig)
    dd = sig * (proj - meas) * inv

    ey0 = 2.0 * jnp.maximum(by0 - ty0 * dd, 0.0) - ys_v[0, 0]
    ey1 = 2.0 * jnp.maximum(by1 - ty1 * dd, 0.0) - ys_v[0, 1]
    ys_v[1, 0] = ey0
    ys_v[1, 1] = ey1
    settled = len(copies)
    h1 = send_y(1)

    def spread(vec, e):
        turned = pltpu.roll(vec, Y - e * Z, 1) if e else vec
        high = turned.astype(jnp.bfloat16).astype(F32)
        parts = [
            jnp.where(chosen, jnp.concatenate([p] * Z, axis=0), 0.0).astype(jnp.bfloat16)
            for p in (high, turned - high)
        ]
        return times_ones(parts).reshape(Z, X, Y)

    def x_half(i):
        part = pl.ds(i * (K // 2), K // 2)
        for side, row in ((0, 0), (1, X - 1)):
            xs_v[1, side, part, :] = ext_v[pl.ds(i * (ROWS // 2) + row, K // 2, stride=X), :]
        lo, hi = (M_X, M_X + 1) if i else (M_H1, M_H1 + 1)
        return [
            (send(xs_v.at[1, 0, part], xr_v.at[1, 1, part], hi, b_lo, b > 0), b < nb - 1),
            (send(xs_v.at[1, 1, part], xr_v.at[1, 0, part], lo, b_hi, b < nb - 1), b > 0),
        ]

    image = jnp.zeros((X, Y), F32)
    for e in range(E):
        u = jnp.maximum(blk(base_v, e) - blk(tw_v, e) * spread(dd, e), 0.0)
        ext = 2.0 * u - blk(maps_v, e)
        put(u_v, e, u)
        put(ext_v, e, ext)
        if e == E // 2 - 1:
            h1 += x_half(0)
        image = image + compact(e, jnp.sum(blk(w_v, e) * ext, axis=2, keepdims=True))
    c_g[me] = image
    c_cp = [send(c_g.at[me], c_g.at[me], M_C + i, p_to[i]) for i in (1, 0, 2)]
    h1 += x_half(1)
    pack_z(ext_v, 1)
    h1 += send_z(1)

    def rows_out(ref, v):
        for e in range(E):
            turned = pltpu.roll(v, Y - e * Z, 1) if e else v
            ref[pl.ds(e * X, X), :] = turned[:, :Z]

    rows_out(emis_o, proj * (1.0 / ny))

    for e in range(E):
        adj, _, _, _ = interior(blk(ext_v, e), (px_v, py_v, pz_v), e)
        put(base_v, e, blk(u_v, e) - blk(tau_v, e) * adj)

    drain(copies[:settled])
    q1 = faces(1, h1, (qx_v[0], qx_v[1], zs_v[2, 0], zs_v[2, 1]) + qy0)
    qx_v[0] = q1[0]
    qx_v[1] = q1[1]
    for e in range(E):
        put(base_v, e, blk(base_v, e) - blk(tau_v, e) * boundary(e, q1))

    for cp in c_cp:
        cp.wait_recv()
    image = (c_g[0] + c_g[1]) + (c_g[2] + c_g[3])
    dd = (dd + sig * (image - meas)) * inv
    for e in range(E):
        put(out_o, e, jnp.maximum(blk(base_v, e) - blk(tw_v, e) * spread(dd, e), 0.0))
    rows_out(dd_o, dd)
    drain(copies[settled:])


def flush(a_ref, b_ref, c_ref, a_o, b_o, c_o, sem):
    parts = [(b_ref.at[pl.ds(i * 256, 256)], b_o.at[pl.ds(i * 256, 256)]) for i in range(4)]
    parts += [(a_ref, a_o), (c_ref, c_o)]
    copies = [pltpu.make_async_copy(src, dst, sem.at[i]) for i, (src, dst) in enumerate(parts)]
    for cp in copies:
        cp.start()
    for cp in copies:
        cp.wait()


def shards(maps, measured, beta_table, view, kappa, line_of, side):
    sizes = tuple(lax.axis_size(a) for a in ("beam", "path", "gz"))
    big = pltpu.VMEM((ROWS, Y), F32)
    scratch = [big] * 12 + [
        pltpu.VMEM((128, Y), F32),
        pltpu.VMEM((E * X, Z), F32),
        pltpu.VMEM((Z, Y), F32),
        pltpu.VMEM((2, Z, Y), F32),
        pltpu.VMEM((Z, Y), F32),
        pltpu.VMEM((Z, Y), F32),
        pltpu.VMEM((3, Z, Y), F32),
        pltpu.VMEM((8, Z, Y), F32),
        pltpu.VMEM((2, Z, Y), F32),
        pltpu.VMEM((Z, Y), F32),
        pltpu.VMEM((2, 2, K, Y), F32),
        pltpu.VMEM((2, 2, K, Y), F32),
        pltpu.VMEM((3, 2, E * X, Y), F32),
        pltpu.VMEM((2, 2, E * X, Y), F32),
        pltpu.VMEM((2, 2, X, Y), F32),
        pltpu.VMEM((2, 2, X, Y), F32),
        pltpu.VMEM((2, K, Y), F32),
        pltpu.VMEM((4, X, Y), F32),
        pltpu.VMEM((4, 2, X, Y), F32),
        pltpu.VMEM((4, X, Y), F32),
        pltpu.SMEM(beta_table.shape, F32),
        pltpu.SMEM(view.shape, jnp.int32),
        pltpu.SMEM(kappa.shape[::-1], F32),
        pltpu.SMEM(line_of.shape, jnp.int32),
        pltpu.SMEM(side.shape, jnp.int32),
        pltpu.SemaphoreType.DMA((E + 6,)),
        pltpu.SemaphoreType.DMA((M_N,)),
        pltpu.SemaphoreType.DMA((M_N,)),
        pltpu.SemaphoreType.REGULAR,
        pltpu.SemaphoreType.REGULAR,
    ]
    emission, out, dual = pl.pallas_call(
        functools.partial(kernel, *sizes),
        out_shape=(
            pltpu.VMEM((E * X, Z), F32),
            pltpu.VMEM((ROWS, Y), F32),
            pltpu.VMEM((E * X, Z), F32),
        ),
        in_specs=[pl.BlockSpec(memory_space=pltpu.HBM)] * 7,
        scratch_shapes=scratch,
        compiler_params=pltpu.CompilerParams(collective_id=0, has_side_effects=True),
        name="xrf",
    )(
        maps.reshape(ROWS, Y),
        measured.transpose(0, 2, 1).reshape(E * X, Z),
        beta_table,
        view,
        kappa.T,
        line_of,
        side,
    )
    hbm = pl.BlockSpec(memory_space=pltpu.HBM)
    vmem = pl.BlockSpec(memory_space=pltpu.VMEM)
    emission, out, dual = pl.pallas_call(
        flush,
        out_shape=tuple(jax.ShapeDtypeStruct(a.shape, F32) for a in (emission, out, dual)),
        in_specs=[vmem] * 3,
        out_specs=(hbm,) * 3,
        scratch_shapes=[pltpu.SemaphoreType.DMA((6,))],
        name="flush",
    )(*(pltpu.with_memory_space_constraint(a, pltpu.VMEM) for a in (emission, out, dual)))
    return (
        emission.reshape(E, X, Z).transpose(0, 2, 1),
        out.reshape(E, Z, X, Y),
        dual.reshape(E, X, Z).transpose(0, 2, 1),
    )


def solution(mesh):
    return jax.shard_map(
        shards,
        mesh=mesh,
        in_specs=(P(None, "gz", "beam", "path"), P(None, "gz", "beam"), P(), P(), P(), P(), P()),
        out_specs=(P(None, "gz", "beam"), P(None, "gz", "beam", "path"), P(None, "gz", "beam")),
        check_vma=False,
    )
```

```python
import functools

import jax
import jax.numpy as jnp
from jax import lax
from jax.experimental import pallas as pl
from jax.experimental.pallas import tpu as pltpu
from jax.sharding import PartitionSpec as P

LAM = 0.1
F32 = jnp.float32
E, Z, X, Y = 8, 16, 8, 128
K = E * Z
ROWS = K * X

M_S = 0
M_CORE = 2
M_V = 3
M_H0 = 11
M_H1 = 17
M_STRIP = 23
M_B = 26
M_C = 29
M_BACK = 32
M_X = 34
M_N = 36
EARLY = 8


def clip(v):
    return jnp.clip(v, -LAM, LAM)


def split2(v):
    hi = v.astype(jnp.bfloat16)
    rest = v - hi.astype(F32)
    mid = rest.astype(jnp.bfloat16)
    return hi, mid


def kernel(
    nb, np_, nz,
    maps_h, meas_h, beta_h, view_h, kappa_h, line_h, side_h,
    emis_o, out_o, dd_o, dc_o, tw_v,
    maps_v, w_v, pre_v, px_v, py_v, pz_v, adj_v, tau_v, base_v, u_v, ext_v, ins_v, meas_v,
    s_v, sr_v, m_v, mr_v, v_v, vr_v, bk_v, att_v,
    xs_v, xr_v, zs_v, zr_v, ys_v, yr_v, qx_v,
    strip_g, b_g, c_g,
    beta_s, view_s, kappa_s, line_s, side_s,
    in_sem, send_sem, recv_sem, far_sem, wrap_sem,
):
    b = lax.axis_index("beam")
    c = lax.div(b, 2)
    k = b - 2 * c
    me = lax.axis_index("path")
    g = lax.axis_index("gz")
    nc = nb // 2
    last = nc - 1

    def chip(d, other=False):
        core = (1 - k) if other else k
        return {"beam": (c + d) * 2 + core}

    def ring(axis, at, n):
        return {axis: jnp.where(at >= n, at - n, at)}

    partner = {"beam": c * 2 + (1 - k)}
    b_lo = {"beam": b - 1}
    b_hi = {"beam": b + 1}
    g_lo = ring("gz", g + nz - 1, nz)
    g_hi = ring("gz", g + 1, nz)
    p_to = [ring("path", me + r, np_) for r in (1, 2, 3)]
    p_lo, p_hi = p_to[2], p_to[0]

    barrier = pltpu.get_barrier_semaphore()

    def greet(p):
        pl.semaphore_signal(barrier, 1, device_id=p)

    def both(d, act, cond):
        @pl.when(cond)
        def _():
            act(chip(d))
            act(chip(d, True))

    for d in (3, 2, 1):
        both(-d, greet, c - d >= 0)
        both(d, greet, c + d <= last)
    both(11, greet, (c >= 2) & (c <= 4))
    both(12, greet, (c >= 1) & (c <= 3))
    for p in p_to + [g_lo, g_hi, partner]:
        greet(p)
    wrapped = c >= last - 2
    met = 6 + 2 * (jnp.minimum(c, 3) + jnp.minimum(last - c, 3))
    met = met + jnp.where(wrapped, 4, 0)

    loads = []
    for i, (src, dst) in enumerate(((beta_h, beta_s), (view_h, view_s))):
        cp = pltpu.make_async_copy(src, dst, in_sem.at[E + 1 + i])
        cp.start()
        loads.append(cp)
    tables = loads
    loads = []
    for e in range(E):
        cp = pltpu.make_async_copy(maps_h.at[pl.ds(e * 128, 128)], maps_v.at[pl.ds(e * 128, 128)], in_sem.at[e])
        cp.start()
        loads.append(cp)
    meas_cp = pltpu.make_async_copy(meas_h, meas_v, in_sem.at[E])
    meas_cp.start()
    lines = []
    for i, (src, dst) in enumerate(((kappa_h, kappa_s), (line_h, line_s), (side_h, side_s))):
        cp = pltpu.make_async_copy(src, dst, in_sem.at[E + 3 + i])
        cp.start()
        lines.append(cp)

    @pl.when(c < 1)
    def _():
        sr_v[0] = jnp.zeros((Z, Y), F32)

    @pl.when(c < 2)
    def _():
        sr_v[1] = jnp.zeros((Z, Y), F32)

    @pl.when(c < 3)
    def _():
        vr_v[0] = jnp.zeros((Z, Y), F32)
        vr_v[1] = jnp.zeros((Z, Y), F32)

    @pl.when(c < EARLY + 3)
    def _():
        vr_v[2] = jnp.zeros((Z, Y), F32)
        vr_v[3] = jnp.zeros((Z, Y), F32)

    @pl.when(c < last - 2)
    def _():
        for i in range(4, 8):
            vr_v[i] = jnp.zeros((Z, Y), F32)

    @pl.when(b == 0)
    def _():
        for it in range(2):
            xr_v[it, 0] = jnp.zeros((K, Y), F32)

    @pl.when(b == nb - 1)
    def _():
        for it in range(2):
            xr_v[it, 1] = jnp.zeros((K, Y), F32)

    copies = []

    def send(src, dst, n, to, cond=None):
        cp = pltpu.make_async_remote_copy(src, dst, send_sem.at[n], recv_sem.at[n], device_id=to)
        if cond is None:
            cp.start()
        else:
            pl.when(cond)(cp.start)
        copies.append((cond, cp))
        return cp

    def drain(some):
        for cond, cp in some:
            if cond is None:
                cp.wait_send()
            else:
                pl.when(cond)(cp.wait_send)

    def arrive(cp, cond=None):
        if cond is None:
            cp.wait_recv()
        else:
            pl.when(cond)(cp.wait_recv)

    lane = lax.broadcasted_iota(jnp.int32, (X, Y), 1)
    sub = lax.broadcasted_iota(jnp.int32, (X, Y), 0)
    lane3 = lax.broadcasted_iota(jnp.int32, (Z, X, Y), 2)
    sub3 = lax.broadcasted_iota(jnp.int32, (Z, X, Y), 1)

    def blk(ref, e):
        return ref[pl.ds(e * 128, 128), :].reshape(Z, X, Y)

    def put(ref, e, v3):
        ref[pl.ds(e * 128, 128), :] = v3.reshape(128, Y)

    def compact(e, r3):
        acc = jnp.zeros((X, Y), F32)
        for z in range(Z):
            acc = jnp.where(lane == e * Z + z, r3[z], acc)
        return acc

    def flag(cond):
        return cond.astype(F32)

    ones = jnp.ones((Y, Y), jnp.bfloat16)
    square = (128, Y)
    chosen = lax.broadcasted_iota(jnp.int32, square, 1) == lax.broadcasted_iota(jnp.int32, square, 0) // X

    def times_ones(parts):
        return sum(jnp.dot(p, ones, preferred_element_type=F32) for p in parts)

    def row_sums(e, v3):
        return compact(e, times_ones(split2(v3.reshape(128, Y))).reshape(Z, X, Y))

    for cp in tables:
        cp.wait()
    acc = None
    for e in range(E):
        loads[e].wait()
        t = blk(maps_v, e) * beta_s[view_s[0], e]
        acc = t if acc is None else acc + t
    slab = jnp.sum(acc, axis=1)
    s_v[...] = slab

    inc = acc
    for sh in (1, 2, 4):
        inc = inc + jnp.where(sub3 >= sh, pltpu.roll(inc, sh, 1), 0.0)
    ins_v[...] = (inc - acc).reshape(128, Y) * (1.0 / (nb * X))

    for cp in lines:
        cp.wait()
    rows = jnp.zeros((X, Y), F32)
    for e in range(E):
        rows = rows + compact(e, jnp.sum(blk(maps_v, e), axis=2, keepdims=True))
    strip = jnp.zeros((X, Y), F32)
    for j in range(E):
        mix = jnp.zeros((X, Y), F32)
        for e in range(E):
            mix = jnp.where(lane // Z == e, kappa_s[(e - j) % E, line_s[e]], mix)
        strip = strip + mix * (pltpu.roll(rows, Z * j, 1) if j else rows)
    strip_g[me] = strip

    def compact_faces(ref):
        lo = jnp.zeros((X, Y), F32)
        hi = jnp.zeros((X, Y), F32)
        for e in range(E):
            v = blk(ref, e)
            lo = lo + compact(e, v[:, :, 0:1])
            hi = hi + compact(e, v[:, :, Y - 1 : Y])
        return lo, hi

    def pack_x(ref, it):
        xs_v[it, 0] = ref[pl.ds(0, K, stride=X), :]
        xs_v[it, 1] = ref[pl.ds(X - 1, K, stride=X), :]

    def pack_z(ref, it):
        for e in range(E):
            zs_v[it, 0, pl.ds(e * X, X), :] = ref[pl.ds(e * 128, X), :]
            zs_v[it, 1, pl.ds(e * X, X), :] = ref[pl.ds(e * 128 + 120, X), :]

    def send_x(it):
        return [
            (send(xs_v.at[it, 0], xr_v.at[it, 1], M_H0 + 6 * it + 1, b_lo, b > 0), b < nb - 1),
            (send(xs_v.at[it, 1], xr_v.at[it, 0], M_H0 + 6 * it + 0, b_hi, b < nb - 1), b > 0),
        ]

    def send_z(it):
        return [
            (send(zs_v.at[it, 0], zr_v.at[it, 1], M_H0 + 6 * it + 3, g_lo), None),
            (send(zs_v.at[it, 1], zr_v.at[it, 0], M_H0 + 6 * it + 2, g_hi), None),
        ]

    def send_y(it):
        return [
            (send(ys_v.at[it, 0], yr_v.at[it, 1], M_H0 + 6 * it + 5, p_lo), None),
            (send(ys_v.at[it, 1], yr_v.at[it, 0], M_H0 + 6 * it + 4, p_hi), None),
        ]

    upper = (
        lax.broadcasted_iota(jnp.int32, (Y, Y), 0) < lax.broadcasted_iota(jnp.int32, (Y, Y), 1)
    ).astype(jnp.bfloat16)

    def absorb(e, _):
        mo = None
        for f in range(E):
            t = maps_v[pl.ds(f * 128, 128), :] * kappa_s[f, line_s[e]]
            mo = t if mo is None else mo + t
        fwd = sum(jnp.dot(part, upper, preferred_element_type=F32) for part in split2(mo))
        far = side_s[e].astype(F32)
        pre_v[pl.ds(pl.multiple_of(e * 128, 128), 128), :] = (1.0 - 2.0 * far) * fwd - far * mo
        return 0

    def interior(v3, p0, e):
        def step(diff, p):
            return clip(0.5 * diff) if p is None else clip(blk(p, e) + 0.5 * diff)

        px = jnp.where(sub3 == X - 1, 0.0, step(pltpu.roll(v3, X - 1, 1) - v3, p0 and p0[0]))
        py = jnp.where(lane3 == Y - 1, 0.0, step(pltpu.roll(v3, Y - 1, 2) - v3, p0 and p0[1]))
        zero = jnp.zeros((1, X, Y), F32)
        diff = jnp.concatenate([v3[1:] - v3[:-1], zero], axis=0)
        pz = step(diff, p0 and p0[2])
        adj = (pltpu.roll(px, 1, 1) - px) + (pltpu.roll(py, 1, 2) - py)
        adj = adj + (jnp.concatenate([zero, pz[:-1]], axis=0) - jnp.concatenate([pz[:-1], zero], axis=0))
        return adj, px, py, pz

    def first_dual(e, _):
        e = pl.multiple_of(e * 128, 128) // 128
        adj, px, py, pz = interior(blk(maps_v, e), None, e)
        put(adj_v, e, adj)
        put(px_v, e, px)
        put(py_v, e, py)
        put(pz_v, e, pz)
        return 0

    def alone():
        lax.fori_loop(0, E, absorb, 0)
        pack_x(maps_v, 0)
        pack_z(maps_v, 0)
        lo, hi = compact_faces(maps_v)
        ys_v[0, 0] = lo
        ys_v[0, 1] = hi
        lax.fori_loop(0, E, first_dual, 0)

    waits = (c >= 1) & (c < EARLY)
    pl.when(waits)(alone)
    pl.semaphore_wait(barrier, met)

    def tell(sem):
        return lambda p: pl.semaphore_signal(sem, 1, device_id=p)

    def windows(src, at, d, cond):
        return [send(v_v.at[src], vr_v.at[at + o], M_V + at + o, chip(d, o == 1), cond) for o in range(2)]

    s_cp = [send(s_v, sr_v.at[i], M_S + i, chip(i + 1), c + i + 1 <= last) for i in (1, 0)]
    s_cp.reverse()
    strip_cp = [send(strip_g.at[me], strip_g.at[me], M_STRIP + i, p_to[i]) for i in (1, 0, 2)]

    @pl.when(c == 0)
    def _():
        v_v[1] = s_v[...]

    windows(1, 0, 3, c == 0)
    both(-3, tell(far_sem), (c >= EARLY) & (c <= last - 3))
    both(-11, tell(wrap_sem), wrapped)
    both(-12, tell(wrap_sem), wrapped)
    back = [send(s_v, bk_v.at[i], M_BACK + i, chip(-i - 1), (c >= 3 + i) & (c <= 5 + i)) for i in range(2)]
    pl.when(~waits)(alone)
    my0, my1 = ys_v[0, 0], ys_v[0, 1]

    for i in range(2):
        arrive(s_cp[i], c >= i + 1)
    near = sr_v[0] + sr_v[1]
    v_v[0] = s_v[...] + near

    three = windows(0, 0, 3, (c >= EARLY) & (c <= last - 3))
    m_v[...] = near + s_v[...] * flag(k == 0)
    m_cp = send(m_v, mr_v, M_CORE, partner)
    h0 = send_x(0) + send_z(0) + send_y(0)

    @pl.when((c >= EARLY - 1) & (c <= last - 6))
    def _():
        pl.semaphore_wait(far_sem, 2)

    six = windows(0, 2, 6, (c >= EARLY - 1) & (c <= last - 6))

    @pl.when(waits)
    def _():
        pl.when(c >= 3)(three[0].wait_recv)
        v_v[1] = v_v[0] + vr_v[0]

    windows(1, 0, 3, waits)

    @pl.when((c >= EARLY - 3) & (c < EARLY - 1))
    def _():
        pl.semaphore_wait(far_sem, 2)

    windows(1, 2, 6, (c >= EARLY - 3) & (c < EARLY - 1))

    for cp in strip_cp:
        cp.wait_recv()
    side_row = jnp.zeros((X, Y), F32)
    for e in range(E):
        side_row = jnp.where(lane // Z == e, side_s[e].astype(F32), side_row)
    below = jnp.zeros((X, Y), F32)
    above = jnp.zeros((X, Y), F32)
    for r in range(4):
        below = below + strip_g[r] * flag(me > r)
        above = above + strip_g[r] * flag(me <= r)
    offset = jnp.where(side_row == 0.0, below, above)
    ny = np_ * Y
    for e in range(E):
        local = blk(pre_v, e)
        ins = ins_v[...].reshape(Z, X, Y)
        parts = []
        for z in range(Z):
            n = e * Z + z
            parts.append(jnp.exp(-(offset[:, n : n + 1] + local[z]) * (1.0 / ny) - ins[z]))
        put(pre_v, e, jnp.stack(parts))

    m_xlo, m_xhi = flag(b > 0), flag(b < nb - 1)
    m_zlo, m_zhi = flag(g > 0), flag(g < nz - 1)
    m_ylo, m_yhi = flag(me > 0), flag(me < np_ - 1)
    ymask = flag(lane == 0) - flag(lane == Y - 1)
    xmask = flag(sub == 0) - flag(sub == X - 1)

    def faces(it, hs, q):
        for cp, cond in hs:
            arrive(cp, cond)
        qx = (
            clip(q[0] + (0.5 * m_xlo) * (xs_v[it, 0] - xr_v[it, 0])),
            clip(q[1] + (0.5 * m_xhi) * (xr_v[it, 1] - xs_v[it, 1])),
        )
        qz = (
            clip(q[2] + (0.5 * m_zlo) * (zs_v[it, 0] - zr_v[it, 0])),
            clip(q[3] + (0.5 * m_zhi) * (zr_v[it, 1] - zs_v[it, 1])),
        )
        qy = (
            clip(q[4] + (0.5 * m_ylo) * (ys_v[it, 0] - yr_v[it, 0])),
            clip(q[5] + (0.5 * m_yhi) * (yr_v[it, 1] - ys_v[it, 1])),
        )
        return qx + qz + qy

    def boundary(e, q):
        shifted = pltpu.roll(q[5], Y - 1, 1)
        even = lax.rem(lane, 2) == 0
        pair = (jnp.where(even, q[4], shifted), jnp.where(even, shifted, q[4]))
        parts = []
        for z in range(Z):
            n = e * Z + z
            r = pair[n % 2]
            if n:
                r = pltpu.roll(r, Y - n, 1)
            lo = jnp.broadcast_to(qx_v[0, pl.ds(n, 1), :], (X, Y))
            hi = jnp.broadcast_to(qx_v[1, pl.ds(n, 1), :], (X, Y))
            t = r * ymask + jnp.where(sub == 0, lo, hi) * xmask
            if z == 0:
                t = t + q[2][e * X : (e + 1) * X]
            if z == Z - 1:
                t = t - q[3][e * X : (e + 1) * X]
            parts.append(t)
        return jnp.stack(parts)

    q0 = faces(0, h0, (0.0,) * 6)
    qx_v[0] = q0[0]
    qx_v[1] = q0[1]
    for e in range(E):
        put(adj_v, e, blk(adj_v, e) + boundary(e, q0))
    qz0 = (q0[2], q0[3])
    qy0 = (q0[4], q0[5])
    zs_v[2, 0] = qz0[0]
    zs_v[2, 1] = qz0[1]

    meas_cp.wait()
    meas = jnp.zeros((X, Y), F32)
    for e in range(E):
        row = jnp.pad(meas_v[pl.ds(e * X, X), :], ((0, 0), (0, Y - Z)))
        meas = meas + (pltpu.roll(row, e * Z, 1) if e else row)

    span = (c >= 2) & (c <= 4)
    whole = (c >= 1) & (c <= 3)

    @pl.when(span)
    def _():
        for cp in back:
            cp.wait_recv()
        v_v[2] = s_v[...] + bk_v[0] + bk_v[1]

    def wrap_sends(at):
        @pl.when(at & (span | whole))
        def _():
            pl.semaphore_wait(wrap_sem, 2 * (span.astype(jnp.int32) + whole.astype(jnp.int32)))

        windows(2, 4, 11, at & span)
        windows(1, 6, 12, at & whole)

    wrap_sends(c >= 3)

    arrive(m_cp)
    arrive(three[0], c >= EARLY)
    arrive(three[1], c >= 3)
    for cp in six:
        arrive(cp, c >= EARLY + 3)

    for i in range(4, 8):
        cp = pltpu.make_async_remote_copy(
            v_v.at[2], vr_v.at[i], send_sem.at[M_V + i], recv_sem.at[M_V + i], device_id=partner
        )
        arrive(cp, wrapped)
    carry = (sr_v[0] + sr_v[1] + mr_v[...]) + (vr_v[0] + vr_v[1]) + (vr_v[2] + vr_v[3])
    carry = carry + ((vr_v[4] + vr_v[5]) + (vr_v[6] + vr_v[7]))
    att_v[...] = jnp.exp(carry * (-1.0 / (nb * X)))
    projs = jnp.zeros((X, Y), F32)
    totals = jnp.zeros((X, Y), F32)
    attb = jnp.stack([jnp.broadcast_to(att_v[pl.ds(z, 1), :], (X, Y)) for z in range(Z)])
    for e in range(E):
        w = blk(pre_v, e) * attb
        put(w_v, e, w)
        totals = totals + row_sums(e, w)
        projs = projs + compact(e, jnp.sum(w * blk(maps_v, e), axis=2, keepdims=True))
    b_g[me, 0] = projs
    b_g[me, 1] = totals
    b_cp = [send(b_g.at[me], b_g.at[me], M_B + i, p_to[i]) for i in (1, 0, 2)]

    wrap_sends(c < 3)

    by0 = jnp.zeros((X, Y), F32)
    by1 = jnp.zeros((X, Y), F32)
    ty0 = jnp.zeros((X, Y), F32)
    ty1 = jnp.zeros((X, Y), F32)
    for e in range(E):
        w = blk(w_v, e)
        tau = 1.0 / (w + 6.0)
        tw = tau * w
        base = blk(maps_v, e) - tau * blk(adj_v, e)
        put(tau_v, e, tau)
        put(tw_v, e, tw)
        put(base_v, e, base)
        by0 = by0 + compact(e, base[:, :, 0:1])
        by1 = by1 + compact(e, base[:, :, Y - 1 : Y])
        ty0 = ty0 + compact(e, tw[:, :, 0:1])
        ty1 = ty1 + compact(e, tw[:, :, Y - 1 : Y])

    for cp in b_cp:
        cp.wait_recv()
    total = (b_g[0] + b_g[1]) + (b_g[2] + b_g[3])
    proj = total[0]
    sig = 1.0 / total[1]
    inv = 1.0 / (1.0 + sig)
    dd = sig * (proj - meas) * inv

    ey0 = 2.0 * jnp.maximum(by0 - ty0 * dd, 0.0) - ys_v[0, 0]
    ey1 = 2.0 * jnp.maximum(by1 - ty1 * dd, 0.0) - ys_v[0, 1]
    ys_v[1, 0] = ey0
    ys_v[1, 1] = ey1
    settled = len(copies)
    h1 = send_y(1)

    def spread(vec, e):
        turned = pltpu.roll(vec, Y - e * Z, 1) if e else vec
        high = turned.astype(jnp.bfloat16).astype(F32)
        parts = [
            jnp.where(chosen, jnp.concatenate([p] * Z, axis=0), 0.0).astype(jnp.bfloat16)
            for p in (high, turned - high)
        ]
        return times_ones(parts).reshape(Z, X, Y)

    def x_half(i):
        part = pl.ds(i * (K // 2), K // 2)
        for side, row in ((0, 0), (1, X - 1)):
            xs_v[1, side, part, :] = ext_v[pl.ds(i * (ROWS // 2) + row, K // 2, stride=X), :]
        lo, hi = (M_X, M_X + 1) if i else (M_H1, M_H1 + 1)
        return [
            (send(xs_v.at[1, 0, part], xr_v.at[1, 1, part], hi, b_lo, b > 0), b < nb - 1),
            (send(xs_v.at[1, 1, part], xr_v.at[1, 0, part], lo, b_hi, b < nb - 1), b > 0),
        ]

    image = jnp.zeros((X, Y), F32)
    for e in range(E):
        u = jnp.maximum(blk(base_v, e) - blk(tw_v, e) * spread(dd, e), 0.0)
        ext = 2.0 * u - blk(maps_v, e)
        put(u_v, e, u)
        put(ext_v, e, ext)
        if e == E // 2 - 1:
            h1 += x_half(0)
        image = image + compact(e, jnp.sum(blk(w_v, e) * ext, axis=2, keepdims=True))
    c_g[me] = image
    c_cp = [send(c_g.at[me], c_g.at[me], M_C + i, p_to[i]) for i in (1, 0, 2)]
    h1 += x_half(1)
    pack_z(ext_v, 1)
    h1 += send_z(1)

    def rows_out(ref, v):
        for e in range(E):
            turned = pltpu.roll(v, Y - e * Z, 1) if e else v
            ref[pl.ds(e * X, X), :] = turned[:, :Z]

    rows_out(emis_o, proj * (1.0 / ny))

    for e in range(E):
        adj, _, _, _ = interior(blk(ext_v, e), (px_v, py_v, pz_v), e)
        put(base_v, e, blk(u_v, e) - blk(tau_v, e) * adj)

    drain(copies[:settled])
    q1 = faces(1, h1, (qx_v[0], qx_v[1], zs_v[2, 0], zs_v[2, 1]) + qy0)
    qx_v[0] = q1[0]
    qx_v[1] = q1[1]
    for e in range(E):
        put(out_o, e, blk(base_v, e) - blk(tau_v, e) * boundary(e, q1))

    for cp in c_cp:
        cp.wait_recv()
    image = (c_g[0] + c_g[1]) + (c_g[2] + c_g[3])
    dd = (dd + sig * (image - meas)) * inv
    dc_o[...] = dd
    rows_out(dd_o, dd)
    drain(copies[settled:])


def flush(a_ref, b_ref, c_ref, d_ref, t_ref, a_o, b_o, c_o, o_v, sem):
    copies = [pltpu.make_async_copy(a_ref, a_o, sem.at[E]), pltpu.make_async_copy(c_ref, c_o, sem.at[E + 1])]
    for cp in copies:
        cp.start()
    ones = jnp.ones((Y, Y), jnp.bfloat16)
    square = (128, Y)
    chosen = lax.broadcasted_iota(jnp.int32, square, 1) == lax.broadcasted_iota(jnp.int32, square, 0) // X
    dual = d_ref[...]
    for e in range(E):
        rows = pl.ds(e * 128, 128)
        turned = pltpu.roll(dual, Y - e * Z, 1) if e else dual
        high = turned.astype(jnp.bfloat16).astype(F32)
        wide = 0.0
        for p in (high, turned - high):
            part = jnp.where(chosen, jnp.concatenate([p] * Z, axis=0), 0.0).astype(jnp.bfloat16)
            wide = wide + jnp.dot(part, ones, preferred_element_type=F32)
        o_v[rows, :] = jnp.maximum(b_ref[rows, :] - t_ref[rows, :] * wide, 0.0)
        cp = pltpu.make_async_copy(o_v.at[rows], b_o.at[rows], sem.at[e])
        cp.start()
        copies.append(cp)
    for cp in copies:
        cp.wait()


def shards(maps, measured, beta_table, view, kappa, line_of, side):
    sizes = tuple(lax.axis_size(a) for a in ("beam", "path", "gz"))
    big = pltpu.VMEM((ROWS, Y), F32)
    scratch = [big] * 11 + [
        pltpu.VMEM((128, Y), F32),
        pltpu.VMEM((E * X, Z), F32),
        pltpu.VMEM((Z, Y), F32),
        pltpu.VMEM((2, Z, Y), F32),
        pltpu.VMEM((Z, Y), F32),
        pltpu.VMEM((Z, Y), F32),
        pltpu.VMEM((3, Z, Y), F32),
        pltpu.VMEM((8, Z, Y), F32),
        pltpu.VMEM((2, Z, Y), F32),
        pltpu.VMEM((Z, Y), F32),
        pltpu.VMEM((2, 2, K, Y), F32),
        pltpu.VMEM((2, 2, K, Y), F32),
        pltpu.VMEM((3, 2, E * X, Y), F32),
        pltpu.VMEM((2, 2, E * X, Y), F32),
        pltpu.VMEM((2, 2, X, Y), F32),
        pltpu.VMEM((2, 2, X, Y), F32),
        pltpu.VMEM((2, K, Y), F32),
        pltpu.VMEM((4, X, Y), F32),
        pltpu.VMEM((4, 2, X, Y), F32),
        pltpu.VMEM((4, X, Y), F32),
        pltpu.SMEM(beta_table.shape, F32),
        pltpu.SMEM(view.shape, jnp.int32),
        pltpu.SMEM(kappa.shape[::-1], F32),
        pltpu.SMEM(line_of.shape, jnp.int32),
        pltpu.SMEM(side.shape, jnp.int32),
        pltpu.SemaphoreType.DMA((E + 6,)),
        pltpu.SemaphoreType.DMA((M_N,)),
        pltpu.SemaphoreType.DMA((M_N,)),
        pltpu.SemaphoreType.REGULAR,
        pltpu.SemaphoreType.REGULAR,
    ]
    emission, out, dual, spare, slope = pl.pallas_call(
        functools.partial(kernel, *sizes),
        out_shape=(
            pltpu.VMEM((E * X, Z), F32),
            pltpu.VMEM((ROWS, Y), F32),
            pltpu.VMEM((E * X, Z), F32),
            pltpu.VMEM((X, Y), F32),
            pltpu.VMEM((ROWS, Y), F32),
        ),
        in_specs=[pl.BlockSpec(memory_space=pltpu.HBM)] * 7,
        scratch_shapes=scratch,
        compiler_params=pltpu.CompilerParams(collective_id=0, has_side_effects=True),
        name="xrf",
    )(
        maps.reshape(ROWS, Y),
        measured.transpose(0, 2, 1).reshape(E * X, Z),
        beta_table,
        view,
        kappa.T,
        line_of,
        side,
    )
    hbm = pl.BlockSpec(memory_space=pltpu.HBM)
    vmem = pl.BlockSpec(memory_space=pltpu.VMEM)
    emission, out, dual = pl.pallas_call(
        flush,
        out_shape=tuple(jax.ShapeDtypeStruct(a.shape, F32) for a in (emission, out, dual)),
        in_specs=[vmem] * 5,
        out_specs=(hbm,) * 3,
        scratch_shapes=[big, pltpu.SemaphoreType.DMA((E + 2,))],
        name="flush",
    )(*(pltpu.with_memory_space_constraint(a, pltpu.VMEM) for a in (emission, out, dual, spare, slope)))
    return (
        emission.reshape(E, X, Z).transpose(0, 2, 1),
        out.reshape(E, Z, X, Y),
        dual.reshape(E, X, Z).transpose(0, 2, 1),
    )


def solution(mesh):
    return jax.shard_map(
        shards,
        mesh=mesh,
        in_specs=(P(None, "gz", "beam", "path"), P(None, "gz", "beam"), P(), P(), P(), P(), P()),
        out_specs=(P(None, "gz", "beam"), P(None, "gz", "beam", "path"), P(None, "gz", "beam")),
        check_vma=False,
    )
```
